256 devices in a mesh: pair: 8 (over y, core), vv: 32 (over x, z).
Axes of the slice: x: 4, y: 4, z: 8, core: 2. Of those that a mesh axis runs over, the one named last changes fastest.
Arguments:
- amplitudes: bfloat16 [1024, 196608], P('pair', 'vv'), may hold values from -6 to 6
- integrals: bfloat16 [96, 32, 24, 128, 128], P('pair', 'vv'), may hold values from -0.01953125 to 0.01953125
- cd_tiles: int32 [96, 32, 24], P('pair', 'vv'), may hold values from 0 to 47
Outputs:
- residual: float32 [1024, 12288], P('vv', 'pair')
The draws below stay inside these ranges and needn't reach their ends.
Inputs may be any that keep to these rules, and one draw needn't show every extreme that they name: cd_tiles counts tiles within the 48 tiles of one index of vv; a tile may appear in several slots of one row tile.
All inputs are finite; a program needn't handle non-finite values.
Results may differ from the reference program's by a relative error of at most 0.0003.
Values may be sent and summed in bfloat16 or wider, within the bound.
No kernel may reach another device: no remote copies, remote signals or barrier semaphores. Data moves between devices by JAX's collectives and lax.ppermute only.
A program may use at most 192 MiB of HBM per device.

```python
import jax
import jax.numpy as jnp
from jax import lax

TILE = 128
CT_DEV = 48
PER_AB = 24
PAIRS = 1024
NB_CD = 1536
NB_AB = 96
N_VV = 32


def place_ends(drawn, stream_key, low, largest):
    longest = drawn.shape.index(max(drawn.shape))
    spots = []
    for shift in (0, 1):
        where = [jax.random.randint(jax.random.fold_in(stream_key, axis), (), 0, length) for axis, length in enumerate(drawn.shape)]
        where[longest] = (where[longest] + shift) % drawn.shape[longest]
        spots.append(tuple(where))
    return drawn.at[spots[0]].set(low).at[spots[1]].set(largest)


def levels(own_key, dims, pieces, least, largest):
    gain, own = 1.0, jax.random.fold_in(own_key, 6)
    for position, blocks in pieces:
        heights = jnp.exp(jax.random.uniform(jax.random.fold_in(own, position), (blocks,), jnp.float32, least / len(pieces), largest / len(pieces)))
        gain = gain * jnp.repeat(heights, dims[position] // blocks).reshape([-1 if axis == position else 1 for axis in range(len(dims))])
    return gain


def centred(key, dims, width, limit, cuts=(), kind=jnp.bfloat16):
    result = width * jax.random.normal(key, dims, jnp.float32)
    if cuts:
        result = result * levels(key, dims, cuts, -0.22, 0.18)
    return jnp.clip(result, -limit, limit).astype(kind)


def setup_inputs(seed: int = 0) -> dict:
    splits = jax.random.split(jax.random.key(seed), 4)
    return {
        "amplitudes": centred(splits[0], (PAIRS, NB_CD * TILE), 1.0, 6.0, ((0, 8), (1, 32))),
        "integrals": centred(splits[1], (NB_AB, N_VV, PER_AB, TILE, TILE), (PER_AB * N_VV * TILE) ** -0.5, 0.01953125, ((0, 8), (1, 32))),
        "cd_tiles": place_ends(jax.random.randint(splits[2], (NB_AB, N_VV, PER_AB), 0, CT_DEV), jax.random.fold_in(splits[2], 1), 0, CT_DEV - 1).astype(jnp.int32),
    }


def reference(amplitudes, integrals, cd_tiles):
    tiled = amplitudes.reshape(PAIRS, NB_CD, TILE)
    offsets = (jnp.arange(N_VV, dtype=jnp.int32) * CT_DEV)[:, None]

    def one_tile(operands):
        blocks, row_tiles = operands
        index = (blocks.astype(jnp.int32) + offsets).reshape(-1).astype(jnp.int32)
        picked = jnp.take(tiled, index, axis=1).astype(jnp.float32)
        weights = row_tiles.reshape(-1, TILE, TILE).astype(jnp.float32)
        return jnp.einsum("pkc,kdc->pd", picked, weights)

    stacked = lax.map(one_tile, (cd_tiles, integrals))
    return jnp.transpose(stacked, (1, 0, 2)).reshape(PAIRS, NB_AB * TILE)
```

```python
import jax
import jax.numpy as jnp
from jax import lax
from jax.experimental import pallas as pl
from jax.experimental.pallas import tpu as pltpu
from jax.sharding import Mesh, PartitionSpec as P

NY, NC, NX, NZ = 4, 2, 4, 8
TILE = 128
ROWS = 32
QW = NY
CHUNKS = ((0, 32),)
LEVELS = 32767.0


def shift(value, axis, size, step):
    return lax.ppermute(value, axis, [(i, (i + step) % size) for i in range(size)])


def encode(total):
    top = jnp.maximum(jnp.max(jnp.abs(total), axis=1, keepdims=True), 1e-30)
    code = jnp.ceil(jnp.log2(top) * 256.0) + 1.0
    scaled = total * (jnp.exp2(code * (-1.0 / 256.0)) * LEVELS)
    return jnp.round(scaled).astype(jnp.int32).astype(jnp.int16), code


def scales(codes):
    return jnp.exp2(codes.astype(jnp.int32).astype(jnp.float32) * (1.0 / 256.0)) * (1.0 / LEVELS)


def contract(pos, cd_tiles, integrals, blocks, height, partial=None):
    n_tiles, n_slots = integrals.shape[0], integrals.shape[1]
    width = n_tiles * TILE
    depth = blocks[0][0].shape[1]
    rows = sum(b[2] for b in blocks)
    step = rows if rows <= 512 else rows // 2
    arrays = []
    for b in blocks:
        if not any(b[0] is a for a in arrays):
            arrays.append(b[0])
    n_arr, n_blk = len(arrays), len(blocks)
    where = [next(i for i, a in enumerate(arrays) if a is b[0]) for b in blocks]
    n_in = 0 if partial is None else 4

    def body(*refs):
        pos_ref, cd_ref = refs[:2]
        w_hbm = refs[2]
        a_hbm = refs[3 : 3 + n_arr]
        outs = refs[3 + n_arr + n_in : 7 + n_arr + n_in]
        wv, av, ov, codes, wsem, asem, osem = refs[7 + n_arr + n_in :]
        starts = []
        at = 0
        for i, b in enumerate(blocks):
            starts.append(at)
            pltpu.make_async_copy(
                a_hbm[where[i]].at[pl.ds(b[1], b[2]), :], av.at[pl.ds(at, b[2]), :], asem.at[i]
            ).start()
            at += b[2]
        for t in range(n_tiles):
            pltpu.make_async_copy(w_hbm.at[t], wv.at[t], wsem.at[t]).start()
        for i, b in enumerate(blocks):
            pltpu.make_async_copy(
                a_hbm[where[i]].at[pl.ds(b[1], b[2]), :], av.at[pl.ds(starts[i], b[2]), :], asem.at[i]
            ).wait()
        codes[...] = jnp.zeros_like(codes)

        def one_tile(t, carry):
            pltpu.make_async_copy(w_hbm.at[t], wv.at[t], wsem.at[t]).wait()
            weights = jnp.concatenate([wv[t, k] for k in range(n_slots)], axis=1)
            for r in range(0, rows, step):
                picked = jnp.concatenate(
                    [
                        av[pl.ds(r, step), pl.ds(pl.multiple_of(cd_ref[t, k] * TILE, TILE), TILE)]
                        for k in range(n_slots)
                    ],
                    axis=1,
                )
                total = lax.dot_general(
                    picked, weights, (((1,), (1,)), ((), ())), preferred_element_type=jnp.float32
                )
                value, code = encode(total)
                ov[pl.ds(r, step), pl.ds(pl.multiple_of(t * TILE, TILE), TILE)] = value
                lane = lax.broadcasted_iota(jnp.int32, (step, TILE), 1)
                codes[pl.ds(r, step), :] = jnp.where(lane == t, code, codes[pl.ds(r, step), :])
            return carry

        lax.fori_loop(0, n_tiles, one_tile, 0)
        ov[:, width:] = codes[...].astype(jnp.int32).astype(jnp.int16)
        y, c, x = pos_ref[0], pos_ref[1], pos_ref[2]
        for i, b in enumerate(blocks):
            slot = (y + b[3] - x + NX) % NX
            first = pl.multiple_of(((c + b[4]) % NC) * (QW * height) + b[5], 8)
            for s in range(NX):

                @pl.when(slot == s)
                def _():
                    pltpu.make_async_copy(
                        ov.at[pl.ds(starts[i], b[2]), :], outs[s].at[pl.ds(first, b[2]), :], osem.at[i]
                    ).start()

        for i, b in enumerate(blocks):
            pltpu.make_async_copy(
                ov.at[pl.ds(starts[i], b[2]), :], outs[0].at[pl.ds(0, b[2]), :], osem.at[i]
            ).wait()

    any_spec = pl.BlockSpec(memory_space=pl.ANY)
    full = jax.ShapeDtypeStruct((NC * QW * height, width + TILE), jnp.int16)
    return pl.pallas_call(
        body,
        out_shape=[full] * 4,
        grid_spec=pltpu.PrefetchScalarGridSpec(
            num_scalar_prefetch=2,
            grid=(1,),
            in_specs=[any_spec] * (1 + n_arr + n_in),
            out_specs=[any_spec] * 4,
            scratch_shapes=[
                pltpu.VMEM(integrals.shape, integrals.dtype),
                pltpu.VMEM((rows, depth), blocks[0][0].dtype),
                pltpu.VMEM((rows, width + TILE), jnp.int16),
                pltpu.VMEM((rows, TILE), jnp.float32),
                pltpu.SemaphoreType.DMA((n_tiles,)),
                pltpu.SemaphoreType.DMA((n_blk,)),
                pltpu.SemaphoreType.DMA((n_blk,)),
            ],
        ),
        input_output_aliases={} if partial is None else {3 + n_arr + s: s for s in range(4)},
        compiler_params=pltpu.CompilerParams(vmem_limit_bytes=48 << 20),
        cost_estimate=pl.CostEstimate(
            flops=4 * rows * n_slots * TILE * width,
            transcendentals=0,
            bytes_accessed=integrals.size * 2 + rows * depth * 2 + rows * width * 2,
        ),
    )(pos, cd_tiles, integrals, *arrays, *(partial or ()))


def add_and_encode(parts, heights):
    wide = parts[0][0].shape[1]
    n_tiles = wide // TILE - 1
    flat = [q for four in parts for q in four]

    def body(*refs):
        out = refs[-1]
        row = 0
        for i, h in enumerate(heights):
            four = refs[4 * i : 4 * i + 4]
            scale = [scales(q[:, n_tiles * TILE :]) for q in four]
            lane = lax.broadcasted_iota(jnp.int32, (h, TILE), 1)
            codes = jnp.zeros((h, TILE), jnp.float32)
            for t in range(n_tiles):
                total = None
                for q, s in zip(four, scale):
                    term = q[:, t * TILE : (t + 1) * TILE].astype(jnp.int32).astype(jnp.float32) * s[:, t : t + 1]
                    total = term if total is None else total + term
                value, code = encode(total)
                out[0, row : row + h, t * TILE : (t + 1) * TILE] = value
                codes = jnp.where(lane == t, code, codes)
            out[0, row : row + h, n_tiles * TILE :] = codes.astype(jnp.int32).astype(jnp.int16)
            row += h

    return pl.pallas_call(
        body,
        out_shape=jax.ShapeDtypeStruct((NZ, sum(heights), wide), jnp.int16),
        grid=(NZ,),
        in_specs=[pl.BlockSpec((h, wide), lambda z: (z, 0)) for h in heights for _ in range(4)],
        out_specs=pl.BlockSpec((1, sum(heights), wide), lambda z: (z, 0, 0)),
    )(*flat)


def add_last(arrived):
    n, rows, wide = arrived.shape
    n_tiles = wide // TILE - 1

    def body(q, out):
        scale = [scales(q[i, :, n_tiles * TILE :]) for i in range(n)]
        for t in range(n_tiles):
            total = None
            for i in range(n):
                term = q[i, :, t * TILE : (t + 1) * TILE].astype(jnp.int32).astype(jnp.float32) * scale[i][:, t : t + 1]
                total = term if total is None else total + term
            out[:, t * TILE : (t + 1) * TILE] = total

    return pl.pallas_call(
        body,
        out_shape=jax.ShapeDtypeStruct((rows, n_tiles * TILE), jnp.float32),
    )(arrived)


def per_device(amplitudes, integrals, cd_tiles):
    integrals = integrals[:, 0]
    cd_tiles = cd_tiles[:, 0]
    depth = amplitudes.shape[1]
    pos = jnp.stack([lax.axis_index("y"), lax.axis_index("c"), lax.axis_index("x")]).astype(jnp.int32)
    other = shift(amplitudes, "c", NC, 1)
    arrived = []
    for first, h in CHUNKS:
        half = QW * h // 2
        if h == ROWS:
            own = amplitudes
        else:
            own = amplitudes.reshape(QW, ROWS, depth)[:, first : first + h].reshape(QW * h, depth)
        up = shift(own, "y", NY, 1)
        down = shift(own, "y", NY, -1)
        far_lo = shift(up[:half], "y", NY, 1)
        far_hi = shift(down[half:], "y", NY, -1)
        up_o, down_o = shift(up, "c", NC, 1), shift(down, "c", NC, 1)
        lo_o, hi_o = shift(far_lo, "c", NC, 1), shift(far_hi, "c", NC, 1)
        early = []
        for source, core in ((amplitudes, 0), (other, 1)):
            for q in range(QW):
                early.append((source, q * ROWS + first, h, 0, core, q * h))
        for up_b, down_b, core in ((up, down, 0), (up_o, down_o, 1)):
            early.append((up_b, 0, QW * h, -1, core, 0))
            early.append((down_b, 0, QW * h, 1, core, 0))
        late = []
        for lo_b, hi_b, core in ((far_lo, far_hi, 0), (lo_o, hi_o, 1)):
            late.append((lo_b, 0, half, 2, core, 0))
            late.append((hi_b, 0, half, 2, core, half))
        coded = contract(pos, cd_tiles, integrals, early, h)
        coded = contract(pos, cd_tiles, integrals, late, h, coded)
        arrived.append([coded[0]] + [shift(coded[s], "x", NX, s) for s in (1, 2, 3)])
    summed = add_and_encode(arrived, [h for _, h in CHUNKS])
    return add_last(lax.all_to_all(summed, "z", 0, 0, tiled=True))


def solution(mesh):
    fine = Mesh(mesh.devices.reshape(NY, NC, NX, NZ), ("y", "c", "x", "z"))
    return jax.shard_map(
        per_device,
        mesh=fine,
        in_specs=(P(("y", "c"), ("x", "z")), P(("y", "c"), ("x", "z")), P(("y", "c"), ("x", "z"))),
        out_specs=P(("x", "z"), ("y", "c")),
        check_vma=False,
    )
```

```python
import jax
import jax.numpy as jnp
from jax import lax
from jax.experimental import pallas as pl
from jax.experimental.pallas import tpu as pltpu
from jax.sharding import Mesh, PartitionSpec as P

NY, NC, NX, NZ = 4, 2, 4, 8
TILE = 128
ROWS = 32
QW = 4
CHUNKS = ((0, 16), (16, 16))
LEVELS = 32767.0


def shift(value, axis, size, step):
    return lax.ppermute(value, axis, [(i, (i + step) % size) for i in range(size)])


def encode(total):
    top = jnp.maximum(jnp.max(jnp.abs(total), axis=1, keepdims=True), 1e-30)
    code = jnp.ceil(jnp.log2(top) * 256.0) + 1.0
    scaled = total * (jnp.exp2(code * (-1.0 / 256.0)) * LEVELS)
    return jnp.round(scaled).astype(jnp.int32).astype(jnp.int16), code


def scales(codes):
    return jnp.exp2(codes.astype(jnp.int32).astype(jnp.float32) * (1.0 / 256.0)) * (1.0 / LEVELS)


def contract(pos, cd_tiles, integrals, blocks, heights, partial=None):
    n_tiles, n_slots = integrals.shape[0], integrals.shape[1]
    width = n_tiles * TILE
    depth = blocks[0][0].shape[1]
    rows = sum(b[2] for b in blocks)
    arrays = []
    for b in blocks:
        if not any(b[0] is a for a in arrays):
            arrays.append(b[0])
    n_arr, n_blk, n_out = len(arrays), len(blocks), 4 * len(heights)
    where = [next(i for i, a in enumerate(arrays) if a is b[0]) for b in blocks]
    starts = [sum(b[2] for b in blocks[:i]) for i in range(n_blk)]
    n_in = 0 if partial is None else n_out

    def body(*refs):
        pos_ref, cd_ref = refs[:2]
        w_hbm = refs[2]
        a_hbm = refs[3 : 3 + n_arr]
        outs = refs[3 + n_arr + n_in : 3 + n_arr + n_in + n_out]
        wv, av, ov, tot, codes, wsem, asem, osem = refs[3 + n_arr + n_in + n_out :]

        def load(i):
            b = blocks[i]
            return pltpu.make_async_copy(
                a_hbm[where[i]].at[pl.ds(b[1], b[2]), :], av.at[pl.ds(starts[i], b[2]), :], asem.at[i]
            )

        def load_weights(t):
            return pltpu.make_async_copy(w_hbm.at[t], wv.at[t], wsem.at[t])

        load_weights(0).start()
        for i in range(n_blk):
            load(i).start()
        for t in range(1, n_tiles):
            load_weights(t).start()
        for i in range(n_blk):
            load(i).wait()
        codes[...] = jnp.zeros_like(codes)
        tot[...] = jnp.zeros_like(tot)
        lane = lax.broadcasted_iota(jnp.int32, (rows, TILE), 1)

        def put(t, column):
            value, code = encode(tot[...])
            ov[:, pl.ds(column, TILE)] = value
            codes[...] = jnp.where(lane == t, code, codes[...])

        def one_tile(t, carry):
            load_weights(t).wait()
            put(t - 1, pl.multiple_of(jnp.maximum(t - 1, 0) * TILE, TILE))
            weights = jnp.concatenate([wv[t, k] for k in range(n_slots)], axis=1)
            picked = jnp.concatenate(
                [av[:, pl.ds(pl.multiple_of(cd_ref[t, k] * TILE, TILE), TILE)] for k in range(n_slots)], axis=1
            )
            tot[...] = lax.dot_general(
                picked, weights, (((1,), (1,)), ((), ())), preferred_element_type=jnp.float32
            )
            return carry

        lax.fori_loop(0, n_tiles, one_tile, 0)
        put(n_tiles - 1, (n_tiles - 1) * TILE)
        ov[:, width:] = codes[...].astype(jnp.int32).astype(jnp.int16)
        y, c, x = pos_ref[0], pos_ref[1], pos_ref[2]
        for i, b in enumerate(blocks):
            slot = (y + b[4] - x + NX) % NX
            first = pl.multiple_of(((c + b[5]) % NC) * (QW * heights[b[3]]) + b[6], 8)
            for s in range(NX):

                @pl.when(slot == s)
                def _():
                    pltpu.make_async_copy(
                        ov.at[pl.ds(starts[i], b[2]), :], outs[4 * b[3] + s].at[pl.ds(first, b[2]), :], osem.at[i]
                    ).start()

        for i, b in enumerate(blocks):
            pltpu.make_async_copy(
                ov.at[pl.ds(starts[i], b[2]), :], outs[4 * b[3]].at[pl.ds(0, b[2]), :], osem.at[i]
            ).wait()

    hbm = pl.BlockSpec(memory_space=pltpu.HBM)
    return pl.pallas_call(
        body,
        out_shape=[
            jax.ShapeDtypeStruct((NC * QW * h, width + TILE), jnp.int16) for h in heights for _ in range(4)
        ],
        grid_spec=pltpu.PrefetchScalarGridSpec(
            num_scalar_prefetch=2,
            grid=(1,),
            in_specs=[hbm] * (1 + n_arr + n_in),
            out_specs=[hbm] * n_out,
            scratch_shapes=[
                pltpu.VMEM(integrals.shape, integrals.dtype),
                pltpu.VMEM((rows, depth), blocks[0][0].dtype),
                pltpu.VMEM((rows, width + TILE), jnp.int16),
                pltpu.VMEM((rows, TILE), jnp.float32),
                pltpu.VMEM((rows, TILE), jnp.float32),
                pltpu.SemaphoreType.DMA((n_tiles,)),
                pltpu.SemaphoreType.DMA((n_blk,)),
                pltpu.SemaphoreType.DMA((n_blk,)),
            ],
        ),
        input_output_aliases={} if partial is None else {3 + n_arr + s: s for s in range(n_out)},
        compiler_params=pltpu.CompilerParams(vmem_limit_bytes=20 << 20),
        cost_estimate=pl.CostEstimate(flops=1, transcendentals=0, bytes_accessed=1),
    )(pos, cd_tiles, integrals, *arrays, *(partial or ()))


def decode(q, scale, tile):
    part = q[:, tile * TILE : (tile + 1) * TILE].astype(jnp.int32).astype(jnp.float32)
    return part * scale[:, tile : tile + 1]


def add_and_encode(pos, parts, h):
    rows, wide = parts[0].shape
    n_tiles = wide // TILE - 1

    def body(pos_ref, *refs):
        four, outs, (scale, codes, res) = refs[:4], refs[4 : 4 + NZ], refs[4 + NZ :]
        lane = lax.broadcasted_iota(jnp.int32, (rows, TILE), 1)
        for i in range(4):
            scale[i] = scales(four[i][:, n_tiles * TILE :])
        codes[...] = jnp.zeros_like(codes)

        def one_tile(t, carry):
            column = pl.ds(pl.multiple_of(t * TILE, TILE), TILE)
            total = None
            for i in range(4):
                factor = jnp.sum(jnp.where(lane == t, scale[i], 0.0), axis=1, keepdims=True)
                part = four[i][:, column].astype(jnp.int32).astype(jnp.float32) * factor
                total = part if total is None else total + part
            value, code = encode(total)
            res[:, column] = value
            codes[...] = jnp.where(lane == t, code, codes[...])
            return carry

        lax.fori_loop(0, n_tiles, one_tile, 0)
        res[:, n_tiles * TILE :] = codes[...].astype(jnp.int32).astype(jnp.int16)
        for s in range(NZ):
            first = pl.multiple_of(((pos_ref[3] + s) % NZ) * h, h)
            outs[s][...] = res[pl.ds(first, h), :]

    vmem = pl.BlockSpec(memory_space=pltpu.VMEM)
    return pl.pallas_call(
        body,
        out_shape=[jax.ShapeDtypeStruct((h, wide), jnp.int16)] * NZ,
        in_specs=[pl.BlockSpec(memory_space=pltpu.SMEM)] + [vmem] * 4,
        out_specs=[vmem] * NZ,
        scratch_shapes=[
            pltpu.VMEM((4, rows, TILE), jnp.float32),
            pltpu.VMEM((rows, TILE), jnp.float32),
            pltpu.VMEM((rows, wide), jnp.int16),
        ],
        compiler_params=pltpu.CompilerParams(vmem_limit_bytes=8 << 20),
    )(pos, *parts)


def add_last(arrived):
    wide = arrived[0][0].shape[1]
    n_tiles = wide // TILE - 1
    heights = [eight[0].shape[0] for eight in arrived]

    def body(*refs):
        out = refs[-1]
        row = 0
        for i, h in enumerate(heights):
            eight = [r[...] for r in refs[NZ * i : NZ * (i + 1)]]
            scale = [scales(q[:, n_tiles * TILE :]) for q in eight]
            for t in range(n_tiles):
                out[row : row + h, t * TILE : (t + 1) * TILE] = sum(decode(q, c, t) for q, c in zip(eight, scale))
            row += h

    return pl.pallas_call(
        body,
        out_shape=jax.ShapeDtypeStruct((sum(heights), n_tiles * TILE), jnp.float32),
        compiler_params=pltpu.CompilerParams(vmem_limit_bytes=8 << 20),
    )(*[q for eight in arrived for q in eight])


def after(values, *others):
    return lax.optimization_barrier((values, others))[0]


def per_device(amplitudes, integrals, cd_tiles):
    integrals = integrals[:, 0]
    cd_tiles = cd_tiles[:, 0]
    depth = amplitudes.shape[1]
    pos = jnp.stack([lax.axis_index(a) for a in ("y", "c", "x", "z")]).astype(jnp.int32)
    heights = [h for _, h in CHUNKS]

    def y_halves(own):
        return shift(own, "y", NY, 1), shift(own, "y", NY, -1)

    def far_halves(up, down):
        half = up.shape[0] // 2
        return shift(up[:half], "y", NY, 1), shift(down[half:], "y", NY, -1)

    def swap(pair):
        return tuple(shift(v, "c", NC, 1) for v in pair)

    def near(i, pair, core):
        up, down = pair
        return [(up, 0, up.shape[0], i, -1, core, 0), (down, 0, down.shape[0], i, 1, core, 0)]

    def far(i, pair, core):
        lo, hi = pair
        return [(lo, 0, lo.shape[0], i, 2, core, 0), (hi, 0, hi.shape[0], i, 2, core, lo.shape[0])]

    parts = [
        amplitudes.reshape(QW, ROWS, depth)[:, first : first + h].reshape(QW * h, depth) for first, h in CHUNKS
    ]
    near_own = [y_halves(parts[0])]
    other = shift(amplitudes, "c", NC, 1)
    blocks = []
    for i, (first, h) in enumerate(CHUNKS):
        for source, core in ((amplitudes, 0), (other, 1)):
            blocks += [(source, q * ROWS + first, h, i, 0, core, q * h) for q in range(QW)]
    coded = contract(pos, cd_tiles, integrals, blocks, heights)
    coded = [coded[4 * i : 4 * i + 4] for i in range(len(CHUNKS))]

    met_x = []
    for i, h in enumerate(heights):
        if i:
            near_own.append(y_halves(after(parts[i], near_other)))
        near_own[i] = after(near_own[i], coded[i])
        far_own = far_halves(*near_own[i])
        near_other = swap(near_own[i])
        blocks = [b for pair, core in ((near_own[i], 0), (near_other, 1)) for b in near(0, pair, core)]
        coded[i] = contract(pos, cd_tiles, integrals, blocks, [h], coded[i])
        far_own = after(far_own, coded[i])
        far_other = swap(far_own)
        if i:
            far_own, met_x[i - 1] = lax.optimization_barrier((far_own, met_x[i - 1]))
        blocks = [b for pair, core in ((far_own, 0), (far_other, 1)) for b in far(0, pair, core)]
        coded[i] = contract(pos, cd_tiles, integrals, blocks, [h], coded[i])
        if i + 1 < len(heights):
            coded[i + 1] = after(coded[i + 1], coded[i])
        met_x.append([coded[i][0]] + [shift(coded[i][s], "x", NX, s) for s in (1, 2, 3)])
    met_z = []
    for i, h in enumerate(heights):
        if i + 1 < len(heights):
            met_x[i] = after(met_x[i], coded[i + 1])
        sums = add_and_encode(pos, met_x[i], h)
        met_z.append([sums[0]] + [shift(sums[s], "z", NZ, s) for s in range(1, NZ)])
    return add_last(met_z)


def solution(mesh):
    fine = Mesh(mesh.devices.reshape(NY, NC, NX, NZ), ("y", "c", "x", "z"))
    return jax.shard_map(
        per_device,
        mesh=fine,
        in_specs=(P(("y", "c"), ("x", "z")), P(("y", "c"), ("x", "z")), P(("y", "c"), ("x", "z"))),
        out_specs=P(("x", "z"), ("y", "c")),
        check_vma=False,
    )
```

```python
import jax
import jax.numpy as jnp
from jax import lax
from jax.experimental import pallas as pl
from jax.experimental.pallas import tpu as pltpu
from jax.sharding import Mesh, PartitionSpec as P

NY, NC, NX, NZ = 4, 2, 4, 8
TILE = 128
ROWS = 32
QW = 4
CHUNKS = ((0, 16), (16, 16))
LEVELS = 32767.0


def shift(value, axis, size, step):
    return lax.ppermute(value, axis, [(i, (i + step) % size) for i in range(size)])


def encode(total):
    top = jnp.maximum(jnp.max(jnp.abs(total), axis=1, keepdims=True), 1e-30)
    code = jnp.ceil(jnp.log2(top) * 256.0) + 1.0
    scaled = total * (jnp.exp2(code * (-1.0 / 256.0)) * LEVELS)
    return jnp.round(scaled).astype(jnp.int32).astype(jnp.int16), code


def scales(codes):
    return jnp.exp2(codes.astype(jnp.int32).astype(jnp.float32) * (1.0 / 256.0)) * (1.0 / LEVELS)


def contract(pos, cd_tiles, integrals, blocks, heights, partial=None):
    n_tiles, n_slots = integrals.shape[0], integrals.shape[1]
    width = n_tiles * TILE
    depth = blocks[0][0].shape[1]
    rows = sum(b[2] for b in blocks)
    arrays = []
    for b in blocks:
        if not any(b[0] is a for a in arrays):
            arrays.append(b[0])
    n_arr, n_blk, n_out = len(arrays), len(blocks), 4 * len(heights)
    where = [next(i for i, a in enumerate(arrays) if a is b[0]) for b in blocks]
    starts = [sum(b[2] for b in blocks[:i]) for i in range(n_blk)]
    n_in = 0 if partial is None else n_out

    def body(*refs):
        pos_ref, cd_ref = refs[:2]
        w_hbm = refs[2]
        a_hbm = refs[3 : 3 + n_arr]
        outs = refs[3 + n_arr + n_in : 3 + n_arr + n_in + n_out]
        wv, av, ov, tot, codes, wsem, asem, osem = refs[3 + n_arr + n_in + n_out :]

        def load(i):
            b = blocks[i]
            return pltpu.make_async_copy(
                a_hbm[where[i]].at[pl.ds(b[1], b[2]), :], av.at[pl.ds(starts[i], b[2]), :], asem.at[i]
            )

        def load_weights(t):
            return pltpu.make_async_copy(w_hbm.at[t], wv.at[t], wsem.at[t])

        load_weights(0).start()
        for i in range(n_blk):
            load(i).start()
        for t in range(1, n_tiles):
            load_weights(t).start()
        for i in range(n_blk):
            load(i).wait()
        codes[...] = jnp.zeros_like(codes)
        tot[...] = jnp.zeros_like(tot)
        lane = lax.broadcasted_iota(jnp.int32, (rows, TILE), 1)

        def put(t, column):
            value, code = encode(tot[...])
            ov[:, pl.ds(column, TILE)] = value
            codes[...] = jnp.where(lane == t, code, codes[...])

        def one_tile(t, carry):
            load_weights(t).wait()
            put(t - 1, pl.multiple_of(jnp.maximum(t - 1, 0) * TILE, TILE))
            weights = jnp.concatenate([wv[t, k] for k in range(n_slots)], axis=1)
            picked = jnp.concatenate(
                [av[:, pl.ds(pl.multiple_of(cd_ref[t, k] * TILE, TILE), TILE)] for k in range(n_slots)], axis=1
            )
            tot[...] = lax.dot_general(
                picked, weights, (((1,), (1,)), ((), ())), preferred_element_type=jnp.float32
            )
            return carry

        lax.fori_loop(0, n_tiles, one_tile, 0)
        put(n_tiles - 1, (n_tiles - 1) * TILE)
        ov[:, width:] = codes[...].astype(jnp.int32).astype(jnp.int16)
        y, c, x = pos_ref[0], pos_ref[1], pos_ref[2]
        for i, b in enumerate(blocks):
            slot = (y + b[4] - x + NX) % NX
            first = pl.multiple_of(((c + b[5]) % NC) * (QW * heights[b[3]]) + b[6], 8)
            for s in range(NX):

                @pl.when(slot == s)
                def _():
                    pltpu.make_async_copy(
                        ov.at[pl.ds(starts[i], b[2]), :], outs[4 * b[3] + s].at[pl.ds(first, b[2]), :], osem.at[i]
                    ).start()

        for i, b in enumerate(blocks):
            pltpu.make_async_copy(
                ov.at[pl.ds(starts[i], b[2]), :], outs[4 * b[3]].at[pl.ds(0, b[2]), :], osem.at[i]
            ).wait()

    hbm = pl.BlockSpec(memory_space=pltpu.HBM)
    return pl.pallas_call(
        body,
        out_shape=[
            jax.ShapeDtypeStruct((NC * QW * h, width + TILE), jnp.int16) for h in heights for _ in range(4)
        ],
        grid_spec=pltpu.PrefetchScalarGridSpec(
            num_scalar_prefetch=2,
            grid=(1,),
            in_specs=[hbm] * (1 + n_arr + n_in),
            out_specs=[hbm] * n_out,
            scratch_shapes=[
                pltpu.VMEM(integrals.shape, integrals.dtype),
                pltpu.VMEM((rows, depth), blocks[0][0].dtype),
                pltpu.VMEM((rows, width + TILE), jnp.int16),
                pltpu.VMEM((rows, TILE), jnp.float32),
                pltpu.VMEM((rows, TILE), jnp.float32),
                pltpu.SemaphoreType.DMA((n_tiles,)),
                pltpu.SemaphoreType.DMA((n_blk,)),
                pltpu.SemaphoreType.DMA((n_blk,)),
            ],
        ),
        input_output_aliases={} if partial is None else {3 + n_arr + s: s for s in range(n_out)},
        compiler_params=pltpu.CompilerParams(vmem_limit_bytes=50 << 20),
        cost_estimate=pl.CostEstimate(flops=1, transcendentals=0, bytes_accessed=1),
    )(pos, cd_tiles, integrals, *arrays, *(partial or ()))


def decode(q, scale, tile):
    part = q[:, tile * TILE : (tile + 1) * TILE].astype(jnp.int32).astype(jnp.float32)
    return part * scale[:, tile : tile + 1]


def column_sum(four, scale, lane, t, column):
    total = None
    for i in range(4):
        factor = jnp.sum(jnp.where(lane == t, scale[i], 0.0), axis=1, keepdims=True)
        part = four[i][:, column].astype(jnp.int32).astype(jnp.float32) * factor
        total = part if total is None else total + part
    return total


def add_plain(parts):
    rows, wide = parts[0].shape
    n_tiles = wide // TILE - 1

    def body(*refs):
        four, out, scale = refs[:4], refs[4], refs[5]
        lane = lax.broadcasted_iota(jnp.int32, (rows, TILE), 1)
        for i in range(4):
            scale[i] = scales(four[i][:, n_tiles * TILE :])

        def one_tile(t, carry):
            column = pl.ds(pl.multiple_of(t * TILE, TILE), TILE)
            out[:, column] = column_sum(four, scale, lane, t, column)
            return carry

        lax.fori_loop(0, n_tiles, one_tile, 0)

    vmem = pl.BlockSpec(memory_space=pltpu.VMEM)
    return pl.pallas_call(
        body,
        out_shape=jax.ShapeDtypeStruct((rows, n_tiles * TILE), jnp.float32),
        in_specs=[vmem] * 4,
        out_specs=vmem,
        scratch_shapes=[pltpu.VMEM((4, rows, TILE), jnp.float32)],
        compiler_params=pltpu.CompilerParams(vmem_limit_bytes=8 << 20),
    )(*parts)


def add_and_encode(pos, parts, h):
    rows, wide = parts[0].shape
    n_tiles = wide // TILE - 1

    def body(pos_ref, *refs):
        four, outs, (scale, codes, res) = refs[:4], refs[4 : 4 + NZ], refs[4 + NZ :]
        lane = lax.broadcasted_iota(jnp.int32, (rows, TILE), 1)
        for i in range(4):
            scale[i] = scales(four[i][:, n_tiles * TILE :])
        codes[...] = jnp.zeros_like(codes)

        def one_tile(t, carry):
            column = pl.ds(pl.multiple_of(t * TILE, TILE), TILE)
            value, code = encode(column_sum(four, scale, lane, t, column))
            res[:, column] = value
            codes[...] = jnp.where(lane == t, code, codes[...])
            return carry

        lax.fori_loop(0, n_tiles, one_tile, 0)
        res[:, n_tiles * TILE :] = codes[...].astype(jnp.int32).astype(jnp.int16)
        for s in range(NZ):
            first = pl.multiple_of(((pos_ref[3] + s) % NZ) * h, h)
            outs[s][...] = res[pl.ds(first, h), :]

    vmem = pl.BlockSpec(memory_space=pltpu.VMEM)
    return pl.pallas_call(
        body,
        out_shape=[jax.ShapeDtypeStruct((h, wide), jnp.int16)] * NZ,
        in_specs=[pl.BlockSpec(memory_space=pltpu.SMEM)] + [vmem] * 4,
        out_specs=[vmem] * NZ,
        scratch_shapes=[
            pltpu.VMEM((4, rows, TILE), jnp.float32),
            pltpu.VMEM((rows, TILE), jnp.float32),
            pltpu.VMEM((rows, wide), jnp.int16),
        ],
        compiler_params=pltpu.CompilerParams(vmem_limit_bytes=8 << 20),
    )(pos, *parts)


def add_last(eight, summed):
    height, wide = eight[0].shape
    n_tiles = wide // TILE - 1
    first = sum(v.shape[0] for v in summed)

    def body(*refs):
        out = refs[-1]
        row = 0
        for r in refs[NZ:-1]:
            out[row : row + r.shape[0], :] = r[...]
            row += r.shape[0]
        parts = [r[...] for r in refs[:NZ]]
        scale = [scales(q[:, n_tiles * TILE :]) for q in parts]
        for t in range(n_tiles):
            out[row:, t * TILE : (t + 1) * TILE] = sum(decode(q, c, t) for q, c in zip(parts, scale))

    return pl.pallas_call(
        body,
        out_shape=jax.ShapeDtypeStruct((first + height, n_tiles * TILE), jnp.float32),
        compiler_params=pltpu.CompilerParams(vmem_limit_bytes=8 << 20),
    )(*eight, *summed)


def after(values, *others):
    return lax.optimization_barrier((values, others))[0]


def per_device(amplitudes, integrals, cd_tiles):
    integrals = integrals[:, 0]
    cd_tiles = cd_tiles[:, 0]
    depth = amplitudes.shape[1]
    pos = jnp.stack([lax.axis_index(a) for a in ("y", "c", "x", "z")]).astype(jnp.int32)
    heights = [h for _, h in CHUNKS]

    def y_halves(own):
        return shift(own, "y", NY, 1), shift(own, "y", NY, -1)

    def far_halves(up, down):
        half = up.shape[0] // 2
        return shift(up[:half], "y", NY, 1), shift(down[half:], "y", NY, -1)

    def swap(pair):
        return tuple(shift(v, "c", NC, 1) for v in pair)

    def near(i, pair, core):
        up, down = pair
        return [(up, 0, up.shape[0], i, -1, core, 0), (down, 0, down.shape[0], i, 1, core, 0)]

    def far(i, pair, core):
        lo, hi = pair
        return [(lo, 0, lo.shape[0], i, 2, core, 0), (hi, 0, hi.shape[0], i, 2, core, lo.shape[0])]

    def rows_of(source, first, h):
        return source.reshape(QW, ROWS, depth)[:, first : first + h].reshape(QW * h, depth)

    near_own = [y_halves(rows_of(amplitudes, *CHUNKS[0]))]
    other = shift(amplitudes, "c", NC, 1)
    blocks = []
    for i, (first, h) in enumerate(CHUNKS):
        for source, core in ((amplitudes, 0), (other, 1)):
            blocks += [(source, q * ROWS + first, h, i, 0, core, q * h) for q in range(QW)]
    coded = contract(pos, cd_tiles, integrals, blocks, heights)
    coded = [coded[4 * i : 4 * i + 4] for i in range(len(CHUNKS))]

    parts = [rows_of(after(amplitudes, coded), *chunk) for chunk in CHUNKS]
    met_x = []
    summed = []
    for i, h in enumerate(heights):
        if i:
            near_own.append(y_halves(after(parts[i], near_other)))
        near_own[i] = after(near_own[i], coded[i])
        far_own = far_halves(*near_own[i])
        near_other = swap(near_own[i])
        blocks = [b for pair, core in ((near_own[i], 0), (near_other, 1)) for b in near(0, pair, core)]
        coded[i] = contract(pos, cd_tiles, integrals, blocks, [h], coded[i])
        far_own = after(far_own, coded[i])
        far_other = swap(far_own)
        if i:
            total = add_plain(after(met_x[i - 1], far_other))
            summed.append(lax.psum_scatter(total, "z", scatter_dimension=0, tiled=True))
            far_own = after(far_own, total)
        blocks = [b for pair, core in ((far_own, 0), (far_other, 1)) for b in far(0, pair, core)]
        coded[i] = contract(pos, cd_tiles, integrals, blocks, [h], coded[i])
        if i + 1 < len(heights):
            coded[i + 1] = after(coded[i + 1], coded[i])
        met_x.append([coded[i][0]] + [shift(coded[i][s], "x", NX, s) for s in (1, 2, 3)])
    sums = add_and_encode(pos, met_x[-1], heights[-1])
    return add_last([sums[0]] + [shift(sums[s], "z", NZ, s) for s in range(1, NZ)], summed)


def solution(mesh):
    fine = Mesh(mesh.devices.reshape(NY, NC, NX, NZ), ("y", "c", "x", "z"))
    return jax.shard_map(
        per_device,
        mesh=fine,
        in_specs=(P(("y", "c"), ("x", "z")), P(("y", "c"), ("x", "z")), P(("y", "c"), ("x", "z"))),
        out_specs=P(("x", "z"), ("y", "c")),
        check_vma=False,
    )
```

```python
import jax
import jax.numpy as jnp
from jax import lax
from jax.experimental import pallas as pl
from jax.experimental.pallas import tpu as pltpu
from jax.sharding import Mesh, PartitionSpec as P

NY, NC, NX, NZ = 4, 2, 4, 8
TILE = 128
ROWS = 32
QW = 4
CHUNKS = (2, 2)
LEVELS = 32767.0


def shift(value, axis, size, step):
    return lax.ppermute(value, axis, [(i, (i + step) % size) for i in range(size)])


def encode(total):
    top = jnp.maximum(jnp.max(jnp.abs(total), axis=1, keepdims=True), 1e-30)
    code = jnp.ceil(jnp.log2(top) * 256.0) + 1.0
    scaled = total * (jnp.exp2(code * (-1.0 / 256.0)) * LEVELS)
    return jnp.round(scaled).astype(jnp.int32).astype(jnp.int16), code


def scales(codes):
    return jnp.exp2(codes.astype(jnp.int32).astype(jnp.float32) * (1.0 / 256.0)) * (1.0 / LEVELS)


def contract(pos, cd_tiles, integrals, blocks, heights, partial=None):
    n_tiles, n_slots = integrals.shape[0], integrals.shape[1]
    width = n_tiles * TILE
    depth = blocks[0][0].shape[1]
    rows = sum(b[2] for b in blocks)
    arrays = []
    for b in blocks:
        if not any(b[0] is a for a in arrays):
            arrays.append(b[0])
    n_arr, n_blk, n_out = len(arrays), len(blocks), 4 * len(heights)
    where = [next(i for i, a in enumerate(arrays) if a is b[0]) for b in blocks]
    starts = [sum(b[2] for b in blocks[:i]) for i in range(n_blk)]
    n_in = 0 if partial is None else n_out

    def body(*refs):
        pos_ref, cd_ref = refs[:2]
        w_hbm = refs[2]
        a_hbm = refs[3 : 3 + n_arr]
        outs = refs[3 + n_arr + n_in : 3 + n_arr + n_in + n_out]
        wv, av, ov, tot, codes, wsem, asem, osem = refs[3 + n_arr + n_in + n_out :]

        def load(i):
            b = blocks[i]
            return pltpu.make_async_copy(
                a_hbm[where[i]].at[pl.ds(b[1], b[2]), :], av.at[pl.ds(starts[i], b[2]), :], asem.at[i]
            )

        def load_weights(t):
            return pltpu.make_async_copy(w_hbm.at[t], wv.at[t], wsem.at[t])

        load_weights(0).start()
        for i in range(n_blk):
            load(i).start()
        for t in range(1, n_tiles):
            load_weights(t).start()
        for i in range(n_blk):
            load(i).wait()
        codes[...] = jnp.zeros_like(codes)
        tot[...] = jnp.zeros_like(tot)
        lane = lax.broadcasted_iota(jnp.int32, (rows, TILE), 1)

        def put(t, column):
            value, code = encode(tot[...])
            ov[:, pl.ds(column, TILE)] = value
            codes[...] = jnp.where(lane == t, code, codes[...])

        def one_tile(t, carry):
            load_weights(t).wait()
            put(t - 1, pl.multiple_of(jnp.maximum(t - 1, 0) * TILE, TILE))
            weights = jnp.concatenate([wv[t, k] for k in range(n_slots)], axis=1)
            picked = jnp.concatenate(
                [av[:, pl.ds(pl.multiple_of(cd_ref[t, k] * TILE, TILE), TILE)] for k in range(n_slots)], axis=1
            )
            tot[...] = lax.dot_general(
                picked, weights, (((1,), (1,)), ((), ())), preferred_element_type=jnp.float32
            )
            return carry

        lax.fori_loop(0, n_tiles, one_tile, 0)
        put(n_tiles - 1, (n_tiles - 1) * TILE)
        ov[:, width:] = codes[...].astype(jnp.int32).astype(jnp.int16)
        y, c, x = pos_ref[0], pos_ref[1], pos_ref[2]
        for i, b in enumerate(blocks):
            slot = (y + b[4] - x + NX) % NX
            first = pl.multiple_of(((c + b[5]) % NC) * heights[b[3]] + b[6], 8)
            for s in range(NX):

                @pl.when(slot == s)
                def _():
                    pltpu.make_async_copy(
                        ov.at[pl.ds(starts[i], b[2]), :], outs[4 * b[3] + s].at[pl.ds(first, b[2]), :], osem.at[i]
                    ).start()

        for i, b in enumerate(blocks):
            pltpu.make_async_copy(
                ov.at[pl.ds(starts[i], b[2]), :], outs[4 * b[3]].at[pl.ds(0, b[2]), :], osem.at[i]
            ).wait()

    hbm = pl.BlockSpec(memory_space=pltpu.HBM)
    return pl.pallas_call(
        body,
        out_shape=[
            jax.ShapeDtypeStruct((NC * h, width + TILE), jnp.int16) for h in heights for _ in range(4)
        ],
        grid_spec=pltpu.PrefetchScalarGridSpec(
            num_scalar_prefetch=2,
            grid=(1,),
            in_specs=[hbm] * (1 + n_arr + n_in),
            out_specs=[hbm] * n_out,
            scratch_shapes=[
                pltpu.VMEM(integrals.shape, integrals.dtype),
                pltpu.VMEM((rows, depth), blocks[0][0].dtype),
                pltpu.VMEM((rows, width + TILE), jnp.int16),
                pltpu.VMEM((rows, TILE), jnp.float32),
                pltpu.VMEM((rows, TILE), jnp.float32),
                pltpu.SemaphoreType.DMA((n_tiles,)),
                pltpu.SemaphoreType.DMA((n_blk,)),
                pltpu.SemaphoreType.DMA((n_blk,)),
            ],
        ),
        input_output_aliases={} if partial is None else {3 + n_arr + s: s for s in range(n_out)},
        compiler_params=pltpu.CompilerParams(vmem_limit_bytes=20 << 20),
        cost_estimate=pl.CostEstimate(flops=1, transcendentals=0, bytes_accessed=1),
    )(pos, cd_tiles, integrals, *arrays, *(partial or ()))


def add_and_encode(four, scale, codes, res):
    rows, wide = res.shape
    n_tiles = wide // TILE - 1
    lane = lax.broadcasted_iota(jnp.int32, (rows, TILE), 1)
    for i in range(4):
        scale[i] = scales(four[i][:, n_tiles * TILE :])
    codes[...] = jnp.zeros_like(codes)

    def one_tile(t, carry):
        column = pl.ds(pl.multiple_of(t * TILE, TILE), TILE)
        total = None
        for i in range(4):
            factor = jnp.sum(jnp.where(lane == t, scale[i], 0.0), axis=1, keepdims=True)
            part = four[i][:, column].astype(jnp.int32).astype(jnp.float32) * factor
            total = part if total is None else total + part
        value, code = encode(total)
        res[:, column] = value
        codes[...] = jnp.where(lane == t, code, codes[...])
        return carry

    lax.fori_loop(0, n_tiles, one_tile, 0)
    res[:, n_tiles * TILE :] = codes[...].astype(jnp.int32).astype(jnp.int16)


def add_scratch(rows, wide):
    return [pltpu.VMEM((4, rows, TILE), jnp.float32), pltpu.VMEM((rows, TILE), jnp.float32)]


def add_first(parts):
    vmem = pl.BlockSpec(memory_space=pltpu.VMEM)

    def body(*refs):
        add_and_encode(refs[:4], refs[5], refs[6], refs[4])

    return pl.pallas_call(
        body,
        out_shape=jax.ShapeDtypeStruct(parts[0].shape, jnp.int16),
        in_specs=[vmem] * 4,
        out_specs=vmem,
        scratch_shapes=add_scratch(*parts[0].shape),
        compiler_params=pltpu.CompilerParams(vmem_limit_bytes=10 << 20),
    )(*parts)


def add_second(pos, parts, done):
    rows, wide = parts[0].shape
    before, here = done.shape[0] // NC, rows // NC
    vmem = pl.BlockSpec(memory_space=pltpu.VMEM)

    def body(pos_ref, *refs):
        first, outs, (res, both, scale, codes) = refs[4], refs[5 : 5 + NZ], refs[5 + NZ :]
        add_and_encode(refs[:4], scale, codes, res)
        for c in range(NC):
            at = c * (before + here)
            both[at : at + before, :] = first[c * before : (c + 1) * before, :]
            both[at + before : at + before + here, :] = res[c * here : (c + 1) * here, :]
        for s in range(NZ):
            row = pl.multiple_of(((pos_ref[3] + s) % NZ) * ROWS, ROWS)
            outs[s][...] = both[pl.ds(row, ROWS), :]

    return pl.pallas_call(
        body,
        out_shape=[jax.ShapeDtypeStruct((ROWS, wide), jnp.int16)] * NZ,
        in_specs=[pl.BlockSpec(memory_space=pltpu.SMEM)] + [vmem] * 5,
        out_specs=[vmem] * NZ,
        scratch_shapes=[pltpu.VMEM((rows, wide), jnp.int16), pltpu.VMEM((NZ * ROWS, wide), jnp.int16)]
        + add_scratch(rows, wide),
        compiler_params=pltpu.CompilerParams(vmem_limit_bytes=10 << 20),
    )(pos, *parts, done)


def add_last(eight):
    rows, wide = eight[0].shape
    n_tiles = wide // TILE - 1

    def body(*refs):
        out, scale = refs[NZ:]
        lane = lax.broadcasted_iota(jnp.int32, (rows, TILE), 1)
        for i in range(NZ):
            scale[i] = scales(refs[i][:, n_tiles * TILE :])

        def one_tile(t, carry):
            column = pl.ds(pl.multiple_of(t * TILE, TILE), TILE)
            total = None
            for i in range(NZ):
                factor = jnp.sum(jnp.where(lane == t, scale[i], 0.0), axis=1, keepdims=True)
                part = refs[i][:, column].astype(jnp.int32).astype(jnp.float32) * factor
                total = part if total is None else total + part
            out[:, column] = total
            return carry

        lax.fori_loop(0, n_tiles, one_tile, 0)

    return pl.pallas_call(
        body,
        out_shape=jax.ShapeDtypeStruct((rows, n_tiles * TILE), jnp.float32),
        scratch_shapes=[pltpu.VMEM((NZ, rows, TILE), jnp.float32)],
        compiler_params=pltpu.CompilerParams(vmem_limit_bytes=8 << 20),
    )(*eight)


def after(values, *others):
    return lax.optimization_barrier((values, others))[0]


def per_device(amplitudes, integrals, cd_tiles):
    integrals = integrals[:, 0]
    cd_tiles = cd_tiles[:, 0]
    pos = jnp.stack([lax.axis_index(a) for a in ("y", "c", "x", "z")]).astype(jnp.int32)
    heights = [ROWS * n for n in CHUNKS]
    firsts = [0, heights[0]]

    def y_near(own):
        return shift(own, "y", NY, 1), shift(own, "y", NY, -1)

    def y_far(up, down):
        half = up.shape[0] // 2
        return shift(up[:half], "y", NY, 1), shift(down[half:], "y", NY, -1)

    def swap(pair):
        return tuple(shift(v, "c", NC, 1) for v in pair)

    def near(chunk, pair, core):
        up, down = pair
        return [(up, 0, up.shape[0], chunk, -1, core, 0), (down, 0, down.shape[0], chunk, 1, core, 0)]

    def along_x(coded):
        return [coded[0]] + [shift(coded[s], "x", NX, s) for s in (1, 2, 3)]

    def rows_of(source, i):
        return source[firsts[i] : firsts[i] + heights[i]]

    near_1 = y_near(rows_of(amplitudes, 0))
    other = shift(amplitudes, "c", NC, 1)
    blocks = [
        (source, firsts[i], heights[i], i, 0, core, 0) for i in range(2) for source, core in ((amplitudes, 0), (other, 1))
    ]
    coded = contract(pos, cd_tiles, integrals, blocks, heights)
    coded_1, coded_2 = coded[:4], coded[4:]
    part_2 = rows_of(after(amplitudes, coded_1), 1)

    def far(chunk, pair, core):
        lo, hi = pair
        return [(lo, 0, lo.shape[0], chunk, 2, core, 0), (hi, 0, hi.shape[0], chunk, 2, core, lo.shape[0])]

    near_1 = after(near_1, coded_1)
    far_1 = y_far(*near_1)
    near_1_other = swap(near_1)
    near_2 = y_near(after(part_2, near_1_other))
    blocks = near(0, near_1, 0) + near(0, near_1_other, 1)
    coded_1 = contract(pos, cd_tiles, integrals, blocks, heights[:1], coded_1)
    far_1 = after(far_1, coded_1)
    blocks = far(0, far_1, 0) + far(0, swap(far_1), 1)
    coded_1 = contract(pos, cd_tiles, integrals, blocks, heights[:1], coded_1)
    met_1 = along_x(coded_1)

    coded_2 = after(coded_2, coded_1)
    near_2 = after(near_2, coded_1)
    far_2 = y_far(*near_2)
    blocks = near(0, near_2, 0) + near(0, swap(near_2), 1)
    coded_2 = contract(pos, cd_tiles, integrals, blocks, heights[1:], coded_2)
    far_2 = after(far_2, coded_2)
    far_2_other = swap(far_2)
    far_2, met_1 = lax.optimization_barrier((far_2, met_1))
    blocks = far(0, far_2, 0) + far(0, far_2_other, 1)
    coded_2 = contract(pos, cd_tiles, integrals, blocks, heights[1:], coded_2)
    met_2 = along_x(coded_2)

    sums = add_second(pos, met_2, add_first(after(met_1, coded_2)))
    return add_last([sums[0]] + [shift(sums[s], "z", NZ, s) for s in range(1, NZ)])


def solution(mesh):
    fine = Mesh(mesh.devices.reshape(NY, NC, NX, NZ), ("y", "c", "x", "z"))
    return jax.shard_map(
        per_device,
        mesh=fine,
        in_specs=(P(("y", "c"), ("x", "z")), P(("y", "c"), ("x", "z")), P(("y", "c"), ("x", "z"))),
        out_specs=P(("x", "z"), ("y", "c")),
        check_vma=False,
    )
```

```python
import jax
import jax.numpy as jnp
from jax import lax
from jax.experimental import pallas as pl
from jax.experimental.pallas import tpu as pltpu
from jax.sharding import Mesh, PartitionSpec as P

NY, NC, NX, NZ = 4, 2, 4, 8
TILE = 128
ROWS = 32
QW = 4
CHUNKS = (2, 2)
LEVELS = 32767.0


def shift(value, axis, size, step):
    return lax.ppermute(value, axis, [(i, (i + step) % size) for i in range(size)])


def encode(total):
    top = jnp.maximum(jnp.max(jnp.abs(total), axis=1, keepdims=True), 1e-30)
    code = jnp.ceil(jnp.log2(top) * 256.0) + 1.0
    scaled = total * (jnp.exp2(code * (-1.0 / 256.0)) * LEVELS)
    return jnp.round(scaled).astype(jnp.int32).astype(jnp.int16), code


def scales(codes):
    return jnp.exp2(codes.astype(jnp.int32).astype(jnp.float32) * (1.0 / 256.0)) * (1.0 / LEVELS)


def contract(pos, cd_tiles, integrals, blocks, heights, partial=None):
    n_tiles, n_slots = integrals.shape[0], integrals.shape[1]
    width = n_tiles * TILE
    depth = blocks[0][0].shape[1]
    rows = sum(b[2] for b in blocks)
    arrays = []
    for b in blocks:
        if not any(b[0] is a for a in arrays):
            arrays.append(b[0])
    n_arr, n_blk, n_out = len(arrays), len(blocks), 4 * len(heights)
    where = [next(i for i, a in enumerate(arrays) if a is b[0]) for b in blocks]
    starts = [sum(b[2] for b in blocks[:i]) for i in range(n_blk)]
    n_in = 0 if partial is None else n_out

    def body(*refs):
        pos_ref, cd_ref = refs[:2]
        w_hbm = refs[2]
        a_hbm = refs[3 : 3 + n_arr]
        outs = refs[3 + n_arr + n_in : 3 + n_arr + n_in + n_out]
        wv, av, ov, tot, codes, wsem, asem, osem = refs[3 + n_arr + n_in + n_out :]

        def load(i):
            b = blocks[i]
            return pltpu.make_async_copy(
                a_hbm[where[i]].at[pl.ds(b[1], b[2]), :], av.at[pl.ds(starts[i], b[2]), :], asem.at[i]
            )

        def load_weights(t):
            return pltpu.make_async_copy(w_hbm.at[t], wv.at[t], wsem.at[t])

        load_weights(0).start()
        for i in range(n_blk):
            load(i).start()
        for t in range(1, n_tiles):
            load_weights(t).start()
        for i in range(n_blk):
            load(i).wait()
        codes[...] = jnp.zeros_like(codes)
        tot[...] = jnp.zeros_like(tot)
        lane = lax.broadcasted_iota(jnp.int32, (rows, TILE), 1)

        def put(t, column):
            value, code = encode(tot[...])
            ov[:, pl.ds(column, TILE)] = value
            codes[...] = jnp.where(lane == t, code, codes[...])

        def one_tile(t, carry):
            load_weights(t).wait()
            put(t - 1, pl.multiple_of(jnp.maximum(t - 1, 0) * TILE, TILE))
            weights = jnp.concatenate([wv[t, k] for k in range(n_slots)], axis=1)
            picked = jnp.concatenate(
                [av[:, pl.ds(pl.multiple_of(cd_ref[t, k] * TILE, TILE), TILE)] for k in range(n_slots)], axis=1
            )
            tot[...] = lax.dot_general(
                picked, weights, (((1,), (1,)), ((), ())), preferred_element_type=jnp.float32
            )
            return carry

        lax.fori_loop(0, n_tiles, one_tile, 0)
        put(n_tiles - 1, (n_tiles - 1) * TILE)
        ov[:, width:] = codes[...].astype(jnp.int32).astype(jnp.int16)
        y, c, x = pos_ref[0], pos_ref[1], pos_ref[2]
        for i, b in enumerate(blocks):
            slot = (y + b[4] - x + NX) % NX
            first = pl.multiple_of(((c + b[5]) % NC) * heights[b[3]] + b[6], 8)
            for s in range(NX):

                @pl.when(slot == s)
                def _():
                    pltpu.make_async_copy(
                        ov.at[pl.ds(starts[i], b[2]), :], outs[4 * b[3] + s].at[pl.ds(first, b[2]), :], osem.at[i]
                    ).start()

        for i, b in enumerate(blocks):
            pltpu.make_async_copy(
                ov.at[pl.ds(starts[i], b[2]), :], outs[4 * b[3]].at[pl.ds(0, b[2]), :], osem.at[i]
            ).wait()

    hbm = pl.BlockSpec(memory_space=pltpu.HBM)
    return pl.pallas_call(
        body,
        out_shape=[
            jax.ShapeDtypeStruct((NC * h, width + TILE), jnp.int16) for h in heights for _ in range(4)
        ],
        grid_spec=pltpu.PrefetchScalarGridSpec(
            num_scalar_prefetch=2,
            grid=(1,),
            in_specs=[hbm] * (1 + n_arr + n_in),
            out_specs=[hbm] * n_out,
            scratch_shapes=[
                pltpu.VMEM(integrals.shape, integrals.dtype),
                pltpu.VMEM((rows, depth), blocks[0][0].dtype),
                pltpu.VMEM((rows, width + TILE), jnp.int16),
                pltpu.VMEM((rows, TILE), jnp.float32),
                pltpu.VMEM((rows, TILE), jnp.float32),
                pltpu.SemaphoreType.DMA((n_tiles,)),
                pltpu.SemaphoreType.DMA((n_blk,)),
                pltpu.SemaphoreType.DMA((n_blk,)),
            ],
        ),
        input_output_aliases={} if partial is None else {3 + n_arr + s: s for s in range(n_out)},
        compiler_params=pltpu.CompilerParams(vmem_limit_bytes=20 << 20),
        cost_estimate=pl.CostEstimate(flops=1, transcendentals=0, bytes_accessed=1),
    )(pos, cd_tiles, integrals, *arrays, *(partial or ()))


def add_and_encode(four, scale, codes, res):
    rows, wide = res.shape
    n_tiles = wide // TILE - 1
    lane = lax.broadcasted_iota(jnp.int32, (rows, TILE), 1)
    for i in range(4):
        scale[i] = scales(four[i][:, n_tiles * TILE :])
    codes[...] = jnp.zeros_like(codes)

    def one_tile(t, carry):
        column = pl.ds(pl.multiple_of(t * TILE, TILE), TILE)
        total = None
        for i in range(4):
            factor = jnp.sum(jnp.where(lane == t, scale[i], 0.0), axis=1, keepdims=True)
            part = four[i][:, column].astype(jnp.int32).astype(jnp.float32) * factor
            total = part if total is None else total + part
        value, code = encode(total)
        res[:, column] = value
        codes[...] = jnp.where(lane == t, code, codes[...])
        return carry

    lax.fori_loop(0, n_tiles, one_tile, 0, unroll=4)
    res[:, n_tiles * TILE :] = codes[...].astype(jnp.int32).astype(jnp.int16)


def add_scratch(rows, wide):
    return [pltpu.VMEM((4, rows, TILE), jnp.float32), pltpu.VMEM((rows, TILE), jnp.float32)]


def add_first(parts):
    vmem = pl.BlockSpec(memory_space=pltpu.VMEM)

    def body(*refs):
        add_and_encode(refs[:4], refs[5], refs[6], refs[4])

    return pl.pallas_call(
        body,
        out_shape=jax.ShapeDtypeStruct(parts[0].shape, jnp.int16),
        in_specs=[vmem] * 4,
        out_specs=vmem,
        scratch_shapes=add_scratch(*parts[0].shape),
        compiler_params=pltpu.CompilerParams(vmem_limit_bytes=10 << 20),
    )(*parts)


def add_second(pos, parts, done):
    rows, wide = parts[0].shape
    before, here = done.shape[0] // NC, rows // NC
    vmem = pl.BlockSpec(memory_space=pltpu.VMEM)

    def body(pos_ref, *refs):
        first, outs, (res, both, scale, codes) = refs[4], refs[5 : 5 + NZ], refs[5 + NZ :]
        add_and_encode(refs[:4], scale, codes, res)
        for c in range(NC):
            at = c * (before + here)
            both[at : at + before, :] = first[c * before : (c + 1) * before, :]
            both[at + before : at + before + here, :] = res[c * here : (c + 1) * here, :]
        for s in range(NZ):
            row = pl.multiple_of(((pos_ref[3] + s) % NZ) * ROWS, ROWS)
            outs[s][...] = both[pl.ds(row, ROWS), :]

    return pl.pallas_call(
        body,
        out_shape=[jax.ShapeDtypeStruct((ROWS, wide), jnp.int16)] * NZ,
        in_specs=[pl.BlockSpec(memory_space=pltpu.SMEM)] + [vmem] * 5,
        out_specs=[vmem] * NZ,
        scratch_shapes=[pltpu.VMEM((rows, wide), jnp.int16), pltpu.VMEM((NZ * ROWS, wide), jnp.int16)]
        + add_scratch(rows, wide),
        compiler_params=pltpu.CompilerParams(vmem_limit_bytes=10 << 20),
    )(pos, *parts, done)


def add_last(eight):
    rows, wide = eight[0].shape
    n_tiles = wide // TILE - 1

    def body(*refs):
        out, scale = refs[NZ:]
        lane = lax.broadcasted_iota(jnp.int32, (rows, TILE), 1)
        for i in range(NZ):
            scale[i] = scales(refs[i][:, n_tiles * TILE :])

        def one_tile(t, carry):
            column = pl.ds(pl.multiple_of(t * TILE, TILE), TILE)
            total = None
            for i in range(NZ):
                factor = jnp.sum(jnp.where(lane == t, scale[i], 0.0), axis=1, keepdims=True)
                part = refs[i][:, column].astype(jnp.int32).astype(jnp.float32) * factor
                total = part if total is None else total + part
            out[:, column] = total
            return carry

        lax.fori_loop(0, n_tiles, one_tile, 0, unroll=4)

    return pl.pallas_call(
        body,
        out_shape=jax.ShapeDtypeStruct((rows, n_tiles * TILE), jnp.float32),
        scratch_shapes=[pltpu.VMEM((NZ, rows, TILE), jnp.float32)],
        compiler_params=pltpu.CompilerParams(vmem_limit_bytes=8 << 20),
    )(*eight)


def after(values, *others):
    return lax.optimization_barrier((values, others))[0]


def per_device(amplitudes, integrals, cd_tiles):
    integrals = integrals[:, 0]
    cd_tiles = cd_tiles[:, 0]
    pos = jnp.stack([lax.axis_index(a) for a in ("y", "c", "x", "z")]).astype(jnp.int32)
    heights = [ROWS * n for n in CHUNKS]
    firsts = [0, heights[0]]

    def y_near(own):
        return shift(own, "y", NY, 1), shift(own, "y", NY, -1)

    def y_far(up, down):
        half = up.shape[0] // 2
        return shift(up[:half], "y", NY, 1), shift(down[half:], "y", NY, -1)

    def swap(pair):
        return tuple(shift(v, "c", NC, 1) for v in pair)

    def near(chunk, pair, core):
        up, down = pair
        return [(up, 0, up.shape[0], chunk, -1, core, 0), (down, 0, down.shape[0], chunk, 1, core, 0)]

    def along_x(coded):
        return [coded[0]] + [shift(coded[s], "x", NX, s) for s in (2, 1, 3)]

    def rows_of(source, i):
        return source[firsts[i] : firsts[i] + heights[i]]

    near_1 = y_near(rows_of(amplitudes, 0))
    other = shift(amplitudes, "c", NC, 1)
    blocks = [
        (source, firsts[i], heights[i], i, 0, core, 0) for i in range(2) for source, core in ((amplitudes, 0), (other, 1))
    ]
    coded = contract(pos, cd_tiles, integrals, blocks, heights)
    coded_1, coded_2 = coded[:4], coded[4:]
    part_2 = rows_of(after(amplitudes, coded_1), 1)

    def far(chunk, pair, core):
        lo, hi = pair
        return [(lo, 0, lo.shape[0], chunk, 2, core, 0), (hi, 0, hi.shape[0], chunk, 2, core, lo.shape[0])]

    near_1 = after(near_1, coded_1)
    far_1 = y_far(*near_1)
    near_1_other = swap(near_1)
    near_2 = y_near(after(part_2, near_1_other))
    blocks = near(0, near_1, 0) + near(0, near_1_other, 1)
    coded_1 = contract(pos, cd_tiles, integrals, blocks, heights[:1], coded_1)
    far_1 = after(far_1, coded_1)
    blocks = far(0, far_1, 0) + far(0, swap(far_1), 1)
    coded_1 = contract(pos, cd_tiles, integrals, blocks, heights[:1], coded_1)
    met_1 = along_x(coded_1)

    coded_2 = after(coded_2, coded_1)
    near_2 = after(near_2, coded_1)
    far_2 = y_far(*near_2)
    blocks = near(0, near_2, 0) + near(0, swap(near_2), 1)
    coded_2 = contract(pos, cd_tiles, integrals, blocks, heights[1:], coded_2)
    far_2 = after(far_2, coded_2)
    far_2_other = swap(far_2)
    blocks = far(0, far_2, 0) + far(0, far_2_other, 1)
    coded_2 = contract(pos, cd_tiles, integrals, blocks, heights[1:], coded_2)
    met_2 = along_x(coded_2)

    sums = add_second(pos, met_2, add_first(after(met_1, coded_2)))
    return add_last([sums[0]] + [shift(sums[s], "z", NZ, s) for s in (4, 3, 5, 2, 6, 1, 7)])


def solution(mesh):
    fine = Mesh(mesh.devices.reshape(NY, NC, NX, NZ), ("y", "c", "x", "z"))
    return jax.shard_map(
        per_device,
        mesh=fine,
        in_specs=(P(("y", "c"), ("x", "z")), P(("y", "c"), ("x", "z")), P(("y", "c"), ("x", "z"))),
        out_specs=P(("x", "z"), ("y", "c")),
        check_vma=False,
    )
```

```python
import jax
import jax.numpy as jnp
from jax import lax
from jax.experimental import pallas as pl
from jax.experimental.pallas import tpu as pltpu
from jax.sharding import Mesh, PartitionSpec as P

NY, NC, NX, NZ = 4, 2, 4, 8
TILE = 128
ROWS = 32
QW = 4
CHUNKS = (2, 2)
LEVELS = 32767.0


def shift(value, axis, size, step):
    return lax.ppermute(value, axis, [(i, (i + step) % size) for i in range(size)])


def encode(total):
    top = jnp.maximum(jnp.max(jnp.abs(total), axis=1, keepdims=True), 1e-30)
    code = jnp.ceil(jnp.log2(top) * 256.0) + 1.0
    scaled = total * (jnp.exp2(code * (-1.0 / 256.0)) * LEVELS)
    return jnp.round(scaled).astype(jnp.int32).astype(jnp.int16), code


def scales(codes):
    return jnp.exp2(codes.astype(jnp.int32).astype(jnp.float32) * (1.0 / 256.0)) * (1.0 / LEVELS)


def contract(pos, cd_tiles, integrals, blocks, heights, partial=None):
    n_tiles, n_slots = integrals.shape[0], integrals.shape[1]
    width = n_tiles * TILE
    depth = blocks[0][0].shape[1]
    rows = sum(b[2] for b in blocks)
    arrays = []
    for b in blocks:
        if not any(b[0] is a for a in arrays):
            arrays.append(b[0])
    n_arr, n_blk, n_out = len(arrays), len(blocks), 4 * len(heights)
    where = [next(i for i, a in enumerate(arrays) if a is b[0]) for b in blocks]
    starts = [sum(b[2] for b in blocks[:i]) for i in range(n_blk)]
    n_in = 0 if partial is None else n_out

    def body(*refs):
        pos_ref, cd_ref = refs[:2]
        w_ref = refs[2]
        a_hbm = refs[3 : 3 + n_arr]
        outs = refs[3 + n_arr + n_in : 3 + n_arr + n_in + n_out]
        av, ov, tot, codes, asem, osem = refs[3 + n_arr + n_in + n_out :]

        def load(i):
            b = blocks[i]
            return pltpu.make_async_copy(
                a_hbm[where[i]].at[pl.ds(b[1], b[2]), :], av.at[pl.ds(starts[i], b[2]), :], asem.at[i]
            )

        for i in range(n_blk):
            load(i).start()
        for i in range(n_blk):
            load(i).wait()
        codes[...] = jnp.zeros_like(codes)
        tot[...] = jnp.zeros_like(tot)
        lane = lax.broadcasted_iota(jnp.int32, (rows, TILE), 1)

        def put(t, column):
            value, code = encode(tot[...])
            ov[:, pl.ds(column, TILE)] = value
            codes[...] = jnp.where(lane == t, code, codes[...])

        def one_tile(t, carry):
            put(t - 1, pl.multiple_of(jnp.maximum(t - 1, 0) * TILE, TILE))
            weights = jnp.concatenate([w_ref[t, k] for k in range(n_slots)], axis=1)
            picked = jnp.concatenate(
                [av[:, pl.ds(pl.multiple_of(cd_ref[t, k] * TILE, TILE), TILE)] for k in range(n_slots)], axis=1
            )
            tot[...] = lax.dot_general(
                picked, weights, (((1,), (1,)), ((), ())), preferred_element_type=jnp.float32
            )
            return carry

        lax.fori_loop(0, n_tiles, one_tile, 0)
        put(n_tiles - 1, (n_tiles - 1) * TILE)
        ov[:, width:] = codes[...].astype(jnp.int32).astype(jnp.int16)
        y, c, x = pos_ref[0], pos_ref[1], pos_ref[2]
        for i, b in enumerate(blocks):
            slot = (y + b[4] - x + NX) % NX
            first = pl.multiple_of(((c + b[5]) % NC) * heights[b[3]] + b[6], 8)
            for s in range(NX):

                @pl.when(slot == s)
                def _():
                    pltpu.make_async_copy(
                        ov.at[pl.ds(starts[i], b[2]), :], outs[4 * b[3] + s].at[pl.ds(first, b[2]), :], osem.at[i]
                    ).start()

        for i, b in enumerate(blocks):
            pltpu.make_async_copy(
                ov.at[pl.ds(starts[i], b[2]), :], outs[4 * b[3]].at[pl.ds(0, b[2]), :], osem.at[i]
            ).wait()

    hbm = pl.BlockSpec(memory_space=pltpu.HBM)
    return pl.pallas_call(
        body,
        out_shape=[
            jax.ShapeDtypeStruct((NC * h, width + TILE), jnp.int16) for h in heights for _ in range(4)
        ],
        grid_spec=pltpu.PrefetchScalarGridSpec(
            num_scalar_prefetch=2,
            grid=(1,),
            in_specs=[pl.BlockSpec(memory_space=pltpu.VMEM)] + [hbm] * (n_arr + n_in),
            out_specs=[hbm] * n_out,
            scratch_shapes=[
                pltpu.VMEM((rows, depth), blocks[0][0].dtype),
                pltpu.VMEM((rows, width + TILE), jnp.int16),
                pltpu.VMEM((rows, TILE), jnp.float32),
                pltpu.VMEM((rows, TILE), jnp.float32),
                pltpu.SemaphoreType.DMA((n_blk,)),
                pltpu.SemaphoreType.DMA((n_blk,)),
            ],
        ),
        input_output_aliases={} if partial is None else {3 + n_arr + s: s for s in range(n_out)},
        compiler_params=pltpu.CompilerParams(vmem_limit_bytes=10 << 20),
        cost_estimate=pl.CostEstimate(flops=1, transcendentals=0, bytes_accessed=1),
    )(pos, cd_tiles, integrals, *arrays, *(partial or ()))


def add_and_encode(four, scale, codes, res):
    rows, wide = res.shape
    n_tiles = wide // TILE - 1
    lane = lax.broadcasted_iota(jnp.int32, (rows, TILE), 1)
    for i in range(4):
        scale[i] = scales(four[i][:, n_tiles * TILE :])
    codes[...] = jnp.zeros_like(codes)

    def one_tile(t, carry):
        column = pl.ds(pl.multiple_of(t * TILE, TILE), TILE)
        total = None
        for i in range(4):
            factor = jnp.sum(jnp.where(lane == t, scale[i], 0.0), axis=1, keepdims=True)
            part = four[i][:, column].astype(jnp.int32).astype(jnp.float32) * factor
            total = part if total is None else total + part
        value, code = encode(total)
        res[:, column] = value
        codes[...] = jnp.where(lane == t, code, codes[...])
        return carry

    lax.fori_loop(0, n_tiles, one_tile, 0, unroll=4)
    res[:, n_tiles * TILE :] = codes[...].astype(jnp.int32).astype(jnp.int16)


def add_scratch(rows, wide):
    return [pltpu.VMEM((4, rows, TILE), jnp.float32), pltpu.VMEM((rows, TILE), jnp.float32)]


def add_first(parts):
    vmem = pl.BlockSpec(memory_space=pltpu.VMEM)

    def body(*refs):
        add_and_encode(refs[:4], refs[5], refs[6], refs[4])

    return pl.pallas_call(
        body,
        out_shape=jax.ShapeDtypeStruct(parts[0].shape, jnp.int16),
        in_specs=[vmem] * 4,
        out_specs=vmem,
        scratch_shapes=add_scratch(*parts[0].shape),
        compiler_params=pltpu.CompilerParams(vmem_limit_bytes=10 << 20),
    )(*parts)


def add_second(pos, parts, done):
    rows, wide = parts[0].shape
    before, here = done.shape[0] // NC, rows // NC
    vmem = pl.BlockSpec(memory_space=pltpu.VMEM)

    def body(pos_ref, *refs):
        first, outs, (res, both, scale, codes) = refs[4], refs[5 : 5 + NZ], refs[5 + NZ :]
        add_and_encode(refs[:4], scale, codes, res)
        for c in range(NC):
            at = c * (before + here)
            both[at : at + before, :] = first[c * before : (c + 1) * before, :]
            both[at + before : at + before + here, :] = res[c * here : (c + 1) * here, :]
        for s in range(NZ):
            row = pl.multiple_of(((pos_ref[3] + s) % NZ) * ROWS, ROWS)
            outs[s][...] = both[pl.ds(row, ROWS), :]

    return pl.pallas_call(
        body,
        out_shape=[jax.ShapeDtypeStruct((ROWS, wide), jnp.int16)] * NZ,
        in_specs=[pl.BlockSpec(memory_space=pltpu.SMEM)] + [vmem] * 5,
        out_specs=[vmem] * NZ,
        scratch_shapes=[pltpu.VMEM((rows, wide), jnp.int16), pltpu.VMEM((NZ * ROWS, wide), jnp.int16)]
        + add_scratch(rows, wide),
        compiler_params=pltpu.CompilerParams(vmem_limit_bytes=10 << 20),
    )(pos, *parts, done)


def add_last(eight):
    rows, wide = eight[0].shape
    n_tiles = wide // TILE - 1

    def body(*refs):
        out, scale = refs[NZ:]
        lane = lax.broadcasted_iota(jnp.int32, (rows, TILE), 1)
        for i in range(NZ):
            scale[i] = scales(refs[i][:, n_tiles * TILE :])

        def one_tile(t, carry):
            column = pl.ds(pl.multiple_of(t * TILE, TILE), TILE)
            total = None
            for i in range(NZ):
                factor = jnp.sum(jnp.where(lane == t, scale[i], 0.0), axis=1, keepdims=True)
                part = refs[i][:, column].astype(jnp.int32).astype(jnp.float32) * factor
                total = part if total is None else total + part
            out[:, column] = total
            return carry

        lax.fori_loop(0, n_tiles, one_tile, 0, unroll=4)

    return pl.pallas_call(
        body,
        out_shape=jax.ShapeDtypeStruct((rows, n_tiles * TILE), jnp.float32),
        scratch_shapes=[pltpu.VMEM((NZ, rows, TILE), jnp.float32)],
        compiler_params=pltpu.CompilerParams(vmem_limit_bytes=8 << 20),
    )(*eight)


def after(values, *others):
    return lax.optimization_barrier((values, others))[0]


def per_device(amplitudes, integrals, cd_tiles):
    integrals = integrals[:, 0]
    cd_tiles = cd_tiles[:, 0]
    pos = jnp.stack([lax.axis_index(a) for a in ("y", "c", "x", "z")]).astype(jnp.int32)
    heights = [ROWS * n for n in CHUNKS]
    firsts = [0, heights[0]]

    def y_near(own):
        return shift(own, "y", NY, 1), shift(own, "y", NY, -1)

    def y_far(up, down):
        half = up.shape[0] // 2
        return shift(up[:half], "y", NY, 1), shift(down[half:], "y", NY, -1)

    def swap(pair):
        return tuple(shift(v, "c", NC, 1) for v in pair)

    def near(chunk, pair, core):
        up, down = pair
        return [(up, 0, up.shape[0], chunk, -1, core, 0), (down, 0, down.shape[0], chunk, 1, core, 0)]

    def along_x(coded):
        return [coded[0]] + [shift(coded[s], "x", NX, s) for s in (2, 1, 3)]

    def rows_of(source, i):
        return source[firsts[i] : firsts[i] + heights[i]]

    near_1 = y_near(rows_of(amplitudes, 0))
    other = shift(amplitudes, "c", NC, 1)
    blocks = [
        (source, firsts[i], heights[i], i, 0, core, 0) for i in range(2) for source, core in ((amplitudes, 0), (other, 1))
    ]
    coded = contract(pos, cd_tiles, integrals, blocks, heights)
    coded_1, coded_2 = coded[:4], coded[4:]

    def far(chunk, pair, core):
        lo, hi = pair
        return [(lo, 0, lo.shape[0], chunk, 2, core, 0), (hi, 0, hi.shape[0], chunk, 2, core, lo.shape[0])]

    part_2 = rows_of(after(amplitudes, coded_1), 1)
    near_1 = after(near_1, coded_1)
    far_1 = y_far(*near_1)
    near_1_other = swap(near_1)
    near_2 = y_near(after(part_2, near_1_other))
    blocks = near(0, near_1, 0) + near(0, near_1_other, 1)
    coded_1 = contract(pos, cd_tiles, integrals, blocks, heights[:1], coded_1)
    far_1 = after(far_1, coded_1)
    blocks = far(0, far_1, 0) + far(0, swap(far_1), 1)
    coded_1 = contract(pos, cd_tiles, integrals, blocks, heights[:1], coded_1)
    met_1 = along_x(coded_1)

    coded_2 = after(coded_2, coded_1)
    near_2 = after(near_2, coded_1)
    half = heights[1] // 2
    far_2 = near_2[0][:half], near_2[1][half:]
    near_2_other = swap(after(near_2, far_2))
    far_2 = shift(far_2[0], "y", NY, 1), shift(far_2[1], "y", NY, -1)
    blocks = near(0, near_2, 0) + near(0, near_2_other, 1)
    coded_2 = contract(pos, cd_tiles, integrals, blocks, heights[1:], coded_2)
    far_2 = after(far_2, coded_2)
    far_2_other = swap(far_2)
    blocks = far(0, far_2, 0) + far(0, far_2_other, 1)
    coded_2 = contract(pos, cd_tiles, integrals, blocks, heights[1:], coded_2)
    met_2 = along_x(coded_2)

    sums = add_second(pos, met_2, add_first(after(met_1, coded_2)))
    return add_last([sums[0]] + [shift(sums[s], "z", NZ, s) for s in (4, 3, 5, 2, 6, 1, 7)])


def solution(mesh):
    fine = Mesh(mesh.devices.reshape(NY, NC, NX, NZ), ("y", "c", "x", "z"))
    return jax.shard_map(
        per_device,
        mesh=fine,
        in_specs=(P(("y", "c"), ("x", "z")), P(("y", "c"), ("x", "z")), P(("y", "c"), ("x", "z"))),
        out_specs=P(("x", "z"), ("y", "c")),
        check_vma=False,
    )
```

```python
import jax
import jax.numpy as jnp
from jax import lax
from jax.experimental import pallas as pl
from jax.experimental.pallas import tpu as pltpu
from jax.sharding import Mesh, PartitionSpec as P

NY, NC, NX, NZ = 4, 2, 4, 8
TILE = 128
ROWS = 32
QW = 4
CHUNKS = (2, 2)
LEVELS = 32767.0
FAR_Z = (4, 3, 5)
NEAR_Z = (2, 6, 1, 7)


def shift(value, axis, size, step):
    return lax.ppermute(value, axis, [(i, (i + step) % size) for i in range(size)])


def shift_to(value, axis, size, step, wanted):
    pairs = [(i, (i + step) % size) for i in range(size)]
    return lax.ppermute(value, axis, [p for p in pairs if wanted(p[1])])


def encode(total):
    top = jnp.maximum(jnp.max(jnp.abs(total), axis=1, keepdims=True), 1e-30)
    code = jnp.ceil(jnp.log2(top) * 256.0) + 1.0
    scaled = total * (jnp.exp2(code * (-1.0 / 256.0)) * LEVELS)
    return jnp.round(scaled).astype(jnp.int32).astype(jnp.int16), code


def scales(codes):
    return jnp.exp2(codes.astype(jnp.int32).astype(jnp.float32) * (1.0 / 256.0)) * (1.0 / LEVELS)


def contract(pos, cd_tiles, integrals, blocks, heights, partial=None):
    n_tiles, n_slots = integrals.shape[0], integrals.shape[1]
    width = n_tiles * TILE
    depth = blocks[0][0].shape[1]
    rows = sum(b[2] for b in blocks)
    arrays = []
    for b in blocks:
        if not any(b[0] is a for a in arrays):
            arrays.append(b[0])
    n_arr, n_blk, n_out = len(arrays), len(blocks), 4 * len(heights)
    where = [next(i for i, a in enumerate(arrays) if a is b[0]) for b in blocks]
    starts = [sum(b[2] for b in blocks[:i]) for i in range(n_blk)]
    n_in = 0 if partial is None else n_out

    def body(*refs):
        pos_ref, cd_ref = refs[:2]
        w_ref = refs[2]
        a_hbm = refs[3 : 3 + n_arr]
        outs = refs[3 + n_arr + n_in : 3 + n_arr + n_in + n_out]
        av, ov, tot, codes, asem, osem = refs[3 + n_arr + n_in + n_out :]

        def load(i):
            b = blocks[i]
            return pltpu.make_async_copy(
                a_hbm[where[i]].at[pl.ds(b[1], b[2]), :], av.at[pl.ds(starts[i], b[2]), :], asem.at[i]
            )

        for i in range(n_blk):
            load(i).start()
        for i in range(n_blk):
            load(i).wait()
        codes[...] = jnp.zeros_like(codes)
        tot[...] = jnp.zeros_like(tot)
        lane = lax.broadcasted_iota(jnp.int32, (rows, TILE), 1)

        def put(t, column):
            value, code = encode(tot[...])
            ov[:, pl.ds(column, TILE)] = value
            codes[...] = jnp.where(lane == t, code, codes[...])

        def one_tile(t, carry):
            put(t - 1, pl.multiple_of(jnp.maximum(t - 1, 0) * TILE, TILE))
            weights = jnp.concatenate([w_ref[t, k] for k in range(n_slots)], axis=1)
            picked = jnp.concatenate(
                [av[:, pl.ds(pl.multiple_of(cd_ref[t, k] * TILE, TILE), TILE)] for k in range(n_slots)], axis=1
            )
            tot[...] = lax.dot_general(
                picked, weights, (((1,), (1,)), ((), ())), preferred_element_type=jnp.float32
            )
            return carry

        lax.fori_loop(0, n_tiles, one_tile, 0)
        put(n_tiles - 1, (n_tiles - 1) * TILE)
        ov[:, width:] = codes[...].astype(jnp.int32).astype(jnp.int16)
        y, c, x = pos_ref[0], pos_ref[1], pos_ref[2]
        for i, b in enumerate(blocks):
            slot = (y + b[4] - x + NX) % NX
            first = pl.multiple_of(((c + b[5]) % NC) * heights[b[3]] + b[6], 8)
            for s in range(NX):

                @pl.when(slot == s)
                def _():
                    pltpu.make_async_copy(
                        ov.at[pl.ds(starts[i], b[2]), :], outs[4 * b[3] + s].at[pl.ds(first, b[2]), :], osem.at[i]
                    ).start()

        for i, b in enumerate(blocks):
            pltpu.make_async_copy(
                ov.at[pl.ds(starts[i], b[2]), :], outs[4 * b[3]].at[pl.ds(0, b[2]), :], osem.at[i]
            ).wait()

    hbm = pl.BlockSpec(memory_space=pltpu.HBM)
    return pl.pallas_call(
        body,
        out_shape=[
            jax.ShapeDtypeStruct((NC * h, width + TILE), jnp.int16) for h in heights for _ in range(4)
        ],
        grid_spec=pltpu.PrefetchScalarGridSpec(
            num_scalar_prefetch=2,
            grid=(1,),
            in_specs=[pl.BlockSpec(memory_space=pltpu.VMEM)] + [hbm] * (n_arr + n_in),
            out_specs=[hbm] * n_out,
            scratch_shapes=[
                pltpu.VMEM((rows, depth), blocks[0][0].dtype),
                pltpu.VMEM((rows, width + TILE), jnp.int16),
                pltpu.VMEM((rows, TILE), jnp.float32),
                pltpu.VMEM((rows, TILE), jnp.float32),
                pltpu.SemaphoreType.DMA((n_blk,)),
                pltpu.SemaphoreType.DMA((n_blk,)),
            ],
        ),
        input_output_aliases={} if partial is None else {3 + n_arr + s: s for s in range(n_out)},
        compiler_params=pltpu.CompilerParams(vmem_limit_bytes=10 << 20),
        cost_estimate=pl.CostEstimate(flops=1, transcendentals=0, bytes_accessed=1),
    )(pos, cd_tiles, integrals, *arrays, *(partial or ()))


def add_and_encode(four, scale, codes, res):
    rows, wide = res.shape
    n_tiles = wide // TILE - 1
    lane = lax.broadcasted_iota(jnp.int32, (rows, TILE), 1)
    for i in range(4):
        scale[i] = scales(four[i][:, n_tiles * TILE :])
    codes[...] = jnp.zeros_like(codes)

    def one_tile(t, carry):
        column = pl.ds(pl.multiple_of(t * TILE, TILE), TILE)
        total = None
        for i in range(4):
            factor = jnp.sum(jnp.where(lane == t, scale[i], 0.0), axis=1, keepdims=True)
            part = four[i][:, column].astype(jnp.int32).astype(jnp.float32) * factor
            total = part if total is None else total + part
        value, code = encode(total)
        res[:, column] = value
        codes[...] = jnp.where(lane == t, code, codes[...])
        return carry

    lax.fori_loop(0, n_tiles, one_tile, 0, unroll=4)
    res[:, n_tiles * TILE :] = codes[...].astype(jnp.int32).astype(jnp.int16)


def add_scratch(rows, wide):
    return [pltpu.VMEM((4, rows, TILE), jnp.float32), pltpu.VMEM((rows, TILE), jnp.float32)]


def add_first(pos, parts):
    rows, wide = parts[0].shape
    vmem = pl.BlockSpec(memory_space=pltpu.VMEM)
    n_far, groups = len(FAR_Z), CHUNKS[0]

    def body(pos_ref, *refs):
        res, outs, (scale, codes) = refs[4], refs[5 : 5 + n_far], refs[5 + n_far :]
        add_and_encode(refs[:4], scale, codes, res)
        for out, s in zip(outs, FAR_Z):
            z = (pos_ref[3] + s) % NZ
            row = pl.multiple_of((z // QW * groups + jnp.minimum(z % QW, groups - 1)) * ROWS, ROWS)
            out[...] = res[pl.ds(row, ROWS), :]

    return pl.pallas_call(
        body,
        out_shape=[jax.ShapeDtypeStruct((rows, wide), jnp.int16)]
        + [jax.ShapeDtypeStruct((ROWS, wide), jnp.int16)] * n_far,
        in_specs=[pl.BlockSpec(memory_space=pltpu.SMEM)] + [vmem] * 4,
        out_specs=[vmem] * (1 + n_far),
        scratch_shapes=add_scratch(rows, wide),
        compiler_params=pltpu.CompilerParams(vmem_limit_bytes=10 << 20),
    )(pos, *parts)


def add_second(pos, parts, done):
    rows, wide = parts[0].shape
    before, here = done.shape[0] // NC, rows // NC
    vmem = pl.BlockSpec(memory_space=pltpu.VMEM)

    def body(pos_ref, *refs):
        first, outs, (res, both, scale, codes) = refs[4], refs[5 : 5 + NZ], refs[5 + NZ :]
        add_and_encode(refs[:4], scale, codes, res)
        for c in range(NC):
            at = c * (before + here)
            both[at : at + before, :] = first[c * before : (c + 1) * before, :]
            both[at + before : at + before + here, :] = res[c * here : (c + 1) * here, :]
        for s in range(NZ):
            row = pl.multiple_of(((pos_ref[3] + s) % NZ) * ROWS, ROWS)
            outs[s][...] = both[pl.ds(row, ROWS), :]

    return pl.pallas_call(
        body,
        out_shape=[jax.ShapeDtypeStruct((ROWS, wide), jnp.int16)] * NZ,
        in_specs=[pl.BlockSpec(memory_space=pltpu.SMEM)] + [vmem] * 5,
        out_specs=[vmem] * NZ,
        scratch_shapes=[pltpu.VMEM((rows, wide), jnp.int16), pltpu.VMEM((NZ * ROWS, wide), jnp.int16)]
        + add_scratch(rows, wide),
        compiler_params=pltpu.CompilerParams(vmem_limit_bytes=10 << 20),
    )(pos, *parts, done)


def add_last(arrived):
    rows, wide = arrived[0].shape
    n = len(arrived)
    n_tiles = wide // TILE - 1

    def body(*refs):
        out, scale = refs[n:]
        lane = lax.broadcasted_iota(jnp.int32, (rows, TILE), 1)
        for i in range(n):
            scale[i] = scales(refs[i][:, n_tiles * TILE :])

        def one_tile(t, carry):
            column = pl.ds(pl.multiple_of(t * TILE, TILE), TILE)
            total = None
            for i in range(n):
                factor = jnp.sum(jnp.where(lane == t, scale[i], 0.0), axis=1, keepdims=True)
                part = refs[i][:, column].astype(jnp.int32).astype(jnp.float32) * factor
                total = part if total is None else total + part
            out[:, column] = total
            return carry

        lax.fori_loop(0, n_tiles, one_tile, 0, unroll=4)

    return pl.pallas_call(
        body,
        out_shape=jax.ShapeDtypeStruct((rows, n_tiles * TILE), jnp.float32),
        scratch_shapes=[pltpu.VMEM((n, rows, TILE), jnp.float32)],
        compiler_params=pltpu.CompilerParams(vmem_limit_bytes=8 << 20),
    )(*arrived)


def after(values, *others):
    return lax.optimization_barrier((values, others))[0]


def per_device(amplitudes, integrals, cd_tiles):
    integrals = integrals[:, 0]
    cd_tiles = cd_tiles[:, 0]
    pos = jnp.stack([lax.axis_index(a) for a in ("y", "c", "x", "z")]).astype(jnp.int32)
    heights = [ROWS * n for n in CHUNKS]
    firsts = [0, heights[0]]

    def y_near(own):
        return shift(own, "y", NY, 1), shift(own, "y", NY, -1)

    def y_far(up, down):
        half = up.shape[0] // 2
        return shift(up[:half], "y", NY, 1), shift(down[half:], "y", NY, -1)

    def swap(pair):
        return tuple(shift(v, "c", NC, 1) for v in pair)

    def near(chunk, pair, core):
        up, down = pair
        return [(up, 0, up.shape[0], chunk, -1, core, 0), (down, 0, down.shape[0], chunk, 1, core, 0)]

    def along_x(coded):
        return [coded[0]] + [shift(coded[s], "x", NX, s) for s in (2, 1, 3)]

    def rows_of(source, i):
        return source[firsts[i] : firsts[i] + heights[i]]

    near_1 = y_near(rows_of(amplitudes, 0))
    other = shift(amplitudes, "c", NC, 1)
    blocks = [
        (source, firsts[i], heights[i], i, 0, core, 0) for i in range(2) for source, core in ((amplitudes, 0), (other, 1))
    ]
    coded = contract(pos, cd_tiles, integrals, blocks, heights)
    coded_1, coded_2 = coded[:4], coded[4:]

    def far(chunk, pair, core):
        lo, hi = pair
        return [(lo, 0, lo.shape[0], chunk, 2, core, 0), (hi, 0, hi.shape[0], chunk, 2, core, lo.shape[0])]

    part_2 = rows_of(after(amplitudes, coded_1), 1)
    near_1 = after(near_1, coded_1)
    far_1 = y_far(*near_1)
    near_1_other = swap(near_1)
    near_2 = y_near(after(part_2, near_1_other))
    blocks = near(0, near_1, 0) + near(0, near_1_other, 1)
    coded_1 = contract(pos, cd_tiles, integrals, blocks, heights[:1], coded_1)
    far_1 = after(far_1, coded_1)
    blocks = far(0, far_1, 0) + far(0, swap(far_1), 1)
    coded_1 = contract(pos, cd_tiles, integrals, blocks, heights[:1], coded_1)
    met_1 = along_x(coded_1)

    coded_2 = after(coded_2, coded_1)
    near_2 = after(near_2, coded_1)
    half = heights[1] // 2
    far_2 = near_2[0][:half], near_2[1][half:]
    near_2_other = swap(after(near_2, far_2))
    far_2 = shift(far_2[0], "y", NY, 1), shift(far_2[1], "y", NY, -1)
    blocks = near(0, near_2, 0) + near(0, near_2_other, 1)
    coded_2 = contract(pos, cd_tiles, integrals, blocks, heights[1:], coded_2)
    far_2 = after(far_2, coded_2)
    far_2_other = swap(far_2)
    blocks = far(0, far_2, 0) + far(0, far_2_other, 1)
    coded_2 = contract(pos, cd_tiles, integrals, blocks, heights[1:], coded_2)
    met_2 = along_x(coded_2)

    done = add_first(pos, after(met_1, coded_2))
    early = [
        shift_to(part, "z", NZ, s, lambda z: z % QW < CHUNKS[0]) for part, s in zip(done[1:], FAR_Z)
    ]
    sums = add_second(pos, met_2, done[0])
    late = [shift_to(sums[s], "z", NZ, s, lambda z: z % QW >= CHUNKS[0]) for s in FAR_Z]
    late += [shift(sums[s], "z", NZ, s) for s in NEAR_Z]
    return add_last([sums[0]] + early + late)


def solution(mesh):
    fine = Mesh(mesh.devices.reshape(NY, NC, NX, NZ), ("y", "c", "x", "z"))
    return jax.shard_map(
        per_device,
        mesh=fine,
        in_specs=(P(("y", "c"), ("x", "z")), P(("y", "c"), ("x", "z")), P(("y", "c"), ("x", "z"))),
        out_specs=P(("x", "z"), ("y", "c")),
        check_vma=False,
    )
```

```python
import jax
import jax.numpy as jnp
from jax import lax
from jax.experimental import pallas as pl
from jax.experimental.pallas import tpu as pltpu
from jax.sharding import Mesh, PartitionSpec as P

NY, NC, NX, NZ = 4, 2, 4, 8
TILE = 128
ROWS = 32
QW = 4
CHUNKS = (2, 2)
LEVELS = 32767.0


def shift(value, axis, size, step):
    return lax.ppermute(value, axis, [(i, (i + step) % size) for i in range(size)])


def encode(total):
    top = jnp.maximum(jnp.max(jnp.abs(total), axis=1, keepdims=True), 1e-30)
    code = jnp.ceil(jnp.log2(top) * 256.0) + 1.0
    scaled = total * (jnp.exp2(code * (-1.0 / 256.0)) * LEVELS)
    return jnp.round(scaled).astype(jnp.int32).astype(jnp.int16), code


def scales(codes):
    return jnp.exp2(codes.astype(jnp.int32).astype(jnp.float32) * (1.0 / 256.0)) * (1.0 / LEVELS)


def contract(pos, cd_tiles, integrals, blocks, heights, partial=None):
    n_tiles, n_slots = integrals.shape[0], integrals.shape[1]
    width = n_tiles * TILE
    depth = blocks[0][0].shape[1]
    rows = sum(b[2] for b in blocks)
    arrays = []
    for b in blocks:
        if not any(b[0] is a for a in arrays):
            arrays.append(b[0])
    n_arr, n_blk, n_out = len(arrays), len(blocks), 4 * len(heights)
    where = [next(i for i, a in enumerate(arrays) if a is b[0]) for b in blocks]
    starts = [sum(b[2] for b in blocks[:i]) for i in range(n_blk)]
    n_in = 0 if partial is None else n_out

    def body(*refs):
        pos_ref, cd_ref = refs[:2]
        w_ref = refs[2]
        a_hbm = refs[3 : 3 + n_arr]
        outs = refs[3 + n_arr + n_in : 3 + n_arr + n_in + n_out]
        av, ov, tot, codes, asem, osem = refs[3 + n_arr + n_in + n_out :]

        def load(i):
            b = blocks[i]
            return pltpu.make_async_copy(
                a_hbm[where[i]].at[pl.ds(b[1], b[2]), :], av.at[pl.ds(starts[i], b[2]), :], asem.at[i]
            )

        for i in range(n_blk):
            load(i).start()
        for i in range(n_blk):
            load(i).wait()
        codes[...] = jnp.zeros_like(codes)
        tot[...] = jnp.zeros_like(tot)
        lane = lax.broadcasted_iota(jnp.int32, (rows, TILE), 1)

        def put(t, column):
            value, code = encode(tot[...])
            ov[:, pl.ds(column, TILE)] = value
            codes[...] = jnp.where(lane == t, code, codes[...])

        def one_tile(t, carry):
            put(t - 1, pl.multiple_of(jnp.maximum(t - 1, 0) * TILE, TILE))
            weights = jnp.concatenate([w_ref[t, k] for k in range(n_slots)], axis=1)
            picked = jnp.concatenate(
                [av[:, pl.ds(pl.multiple_of(cd_ref[t, k] * TILE, TILE), TILE)] for k in range(n_slots)], axis=1
            )
            tot[...] = lax.dot_general(
                picked, weights, (((1,), (1,)), ((), ())), preferred_element_type=jnp.float32
            )
            return carry

        lax.fori_loop(0, n_tiles, one_tile, 0)
        put(n_tiles - 1, (n_tiles - 1) * TILE)
        ov[:, width:] = codes[...].astype(jnp.int32).astype(jnp.int16)
        y, c, x = pos_ref[0], pos_ref[1], pos_ref[2]
        for i, b in enumerate(blocks):
            slot = (y + b[4] - x + NX) % NX
            first = pl.multiple_of(((c + b[5]) % NC) * heights[b[3]] + b[6], 8)
            for s in range(NX):

                @pl.when(slot == s)
                def _():
                    pltpu.make_async_copy(
                        ov.at[pl.ds(starts[i], b[2]), :], outs[4 * b[3] + s].at[pl.ds(first, b[2]), :], osem.at[i]
                    ).start()

        for i, b in enumerate(blocks):
            pltpu.make_async_copy(
                ov.at[pl.ds(starts[i], b[2]), :], outs[4 * b[3]].at[pl.ds(0, b[2]), :], osem.at[i]
            ).wait()

    hbm = pl.BlockSpec(memory_space=pltpu.HBM)
    return pl.pallas_call(
        body,
        out_shape=[
            jax.ShapeDtypeStruct((NC * h, width + TILE), jnp.int16) for h in heights for _ in range(4)
        ],
        grid_spec=pltpu.PrefetchScalarGridSpec(
            num_scalar_prefetch=2,
            grid=(1,),
            in_specs=[pl.BlockSpec(memory_space=pltpu.VMEM)] + [hbm] * (n_arr + n_in),
            out_specs=[hbm] * n_out,
            scratch_shapes=[
                pltpu.VMEM((rows, depth), blocks[0][0].dtype),
                pltpu.VMEM((rows, width + TILE), jnp.int16),
                pltpu.VMEM((rows, TILE), jnp.float32),
                pltpu.VMEM((rows, TILE), jnp.float32),
                pltpu.SemaphoreType.DMA((n_blk,)),
                pltpu.SemaphoreType.DMA((n_blk,)),
            ],
        ),
        input_output_aliases={} if partial is None else {3 + n_arr + s: s for s in range(n_out)},
        compiler_params=pltpu.CompilerParams(vmem_limit_bytes=10 << 20),
        cost_estimate=pl.CostEstimate(flops=1, transcendentals=0, bytes_accessed=1),
    )(pos, cd_tiles, integrals, *arrays, *(partial or ()))


def add_and_encode(four, scale, codes, res):
    rows, wide = res.shape
    n_tiles = wide // TILE - 1
    lane = lax.broadcasted_iota(jnp.int32, (rows, TILE), 1)
    for i in range(4):
        scale[i] = scales(four[i][:, n_tiles * TILE :])
    codes[...] = jnp.zeros_like(codes)

    def one_tile(t, carry):
        column = pl.ds(pl.multiple_of(t * TILE, TILE), TILE)
        total = None
        for i in range(4):
            factor = jnp.sum(jnp.where(lane == t, scale[i], 0.0), axis=1, keepdims=True)
            part = four[i][:, column].astype(jnp.int32).astype(jnp.float32) * factor
            total = part if total is None else total + part
        value, code = encode(total)
        res[:, column] = value
        codes[...] = jnp.where(lane == t, code, codes[...])
        return carry

    lax.fori_loop(0, n_tiles, one_tile, 0, unroll=4)
    res[:, n_tiles * TILE :] = codes[...].astype(jnp.int32).astype(jnp.int16)


def add_scratch(rows, wide):
    return [pltpu.VMEM((4, rows, TILE), jnp.float32), pltpu.VMEM((rows, TILE), jnp.float32)]


def add_first(parts):
    vmem = pl.BlockSpec(memory_space=pltpu.VMEM)

    def body(*refs):
        add_and_encode(refs[:4], refs[5], refs[6], refs[4])

    return pl.pallas_call(
        body,
        out_shape=jax.ShapeDtypeStruct(parts[0].shape, jnp.int16),
        in_specs=[vmem] * 4,
        out_specs=vmem,
        scratch_shapes=add_scratch(*parts[0].shape),
        compiler_params=pltpu.CompilerParams(vmem_limit_bytes=10 << 20),
    )(*parts)


def add_second(pos, parts, done):
    rows, wide = parts[0].shape
    before, here = done.shape[0] // NC, rows // NC
    vmem = pl.BlockSpec(memory_space=pltpu.VMEM)

    def body(pos_ref, *refs):
        first, outs, (res, both, scale, codes) = refs[4], refs[5 : 5 + NZ], refs[5 + NZ :]
        add_and_encode(refs[:4], scale, codes, res)
        for c in range(NC):
            at = c * (before + here)
            both[at : at + before, :] = first[c * before : (c + 1) * before, :]
            both[at + before : at + before + here, :] = res[c * here : (c + 1) * here, :]
        for s in range(NZ):
            row = pl.multiple_of(((pos_ref[3] + s) % NZ) * ROWS, ROWS)
            outs[s][...] = both[pl.ds(row, ROWS), :]

    return pl.pallas_call(
        body,
        out_shape=[jax.ShapeDtypeStruct((ROWS, wide), jnp.int16)] * NZ,
        in_specs=[pl.BlockSpec(memory_space=pltpu.SMEM)] + [vmem] * 5,
        out_specs=[vmem] * NZ,
        scratch_shapes=[pltpu.VMEM((rows, wide), jnp.int16), pltpu.VMEM((NZ * ROWS, wide), jnp.int16)]
        + add_scratch(rows, wide),
        compiler_params=pltpu.CompilerParams(vmem_limit_bytes=10 << 20),
    )(pos, *parts, done)


def add_last(eight):
    rows, wide = eight[0].shape
    n_tiles = wide // TILE - 1

    def body(*refs):
        out, scale = refs[NZ:]
        lane = lax.broadcasted_iota(jnp.int32, (rows, TILE), 1)
        for i in range(NZ):
            scale[i] = scales(refs[i][:, n_tiles * TILE :])

        def one_tile(t, carry):
            column = pl.ds(pl.multiple_of(t * TILE, TILE), TILE)
            total = None
            for i in range(NZ):
                factor = jnp.sum(jnp.where(lane == t, scale[i], 0.0), axis=1, keepdims=True)
                part = refs[i][:, column].astype(jnp.int32).astype(jnp.float32) * factor
                total = part if total is None else total + part
            out[:, column] = total
            return carry

        lax.fori_loop(0, n_tiles, one_tile, 0, unroll=4)

    return pl.pallas_call(
        body,
        out_shape=jax.ShapeDtypeStruct((rows, n_tiles * TILE), jnp.float32),
        scratch_shapes=[pltpu.VMEM((NZ, rows, TILE), jnp.float32)],
        compiler_params=pltpu.CompilerParams(vmem_limit_bytes=8 << 20),
    )(*eight)


def after(values, *others):
    return lax.optimization_barrier((values, others))[0]


def per_device(amplitudes, integrals, cd_tiles):
    integrals = integrals[:, 0]
    cd_tiles = cd_tiles[:, 0]
    pos = jnp.stack([lax.axis_index(a) for a in ("y", "c", "x", "z")]).astype(jnp.int32)
    heights = [ROWS * n for n in CHUNKS]
    firsts = [0, heights[0]]

    def y_near(own):
        return shift(own, "y", NY, 1), shift(own, "y", NY, -1)

    def y_far(up, down):
        half = up.shape[0] // 2
        return shift(up[:half], "y", NY, 1), shift(down[half:], "y", NY, -1)

    def swap(pair):
        return tuple(shift(v, "c", NC, 1) for v in pair)

    def near(chunk, pair, core):
        up, down = pair
        return [(up, 0, up.shape[0], chunk, -1, core, 0), (down, 0, down.shape[0], chunk, 1, core, 0)]

    def along_x(coded):
        return [coded[0]] + [shift(coded[s], "x", NX, s) for s in (2, 1, 3)]

    def rows_of(source, i):
        return source[firsts[i] : firsts[i] + heights[i]]

    near_1 = y_near(rows_of(amplitudes, 0))
    other = shift(amplitudes, "c", NC, 1)
    blocks = [
        (source, firsts[i], heights[i], i, 0, core, 0) for i in range(2) for source, core in ((amplitudes, 0), (other, 1))
    ]
    coded = contract(pos, cd_tiles, integrals, blocks, heights)
    coded_1, coded_2 = coded[:4], coded[4:]

    def far(chunk, pair, core):
        lo, hi = pair
        return [(lo, 0, lo.shape[0], chunk, 2, core, 0), (hi, 0, hi.shape[0], chunk, 2, core, lo.shape[0])]

    part_2 = rows_of(after(amplitudes, coded_1), 1)
    near_1 = after(near_1, coded_1)
    far_1 = y_far(*near_1)
    near_1_other = swap(near_1)
    near_2 = y_near(after(part_2, near_1_other))
    blocks = near(0, near_1, 0) + near(0, near_1_other, 1)
    coded_1 = contract(pos, cd_tiles, integrals, blocks, heights[:1], coded_1)
    far_1 = after(far_1, coded_1)
    blocks = far(0, far_1, 0) + far(0, swap(far_1), 1)
    coded_1 = contract(pos, cd_tiles, integrals, blocks, heights[:1], coded_1)
    met_1 = along_x(coded_1)

    coded_2 = after(coded_2, coded_1)
    near_2 = after(near_2, coded_1)
    half = heights[1] // 2
    far_2 = near_2[0][:half], near_2[1][half:]
    near_2_other = swap(after(near_2, far_2))
    far_2 = shift(far_2[0], "y", NY, 1), shift(far_2[1], "y", NY, -1)
    blocks = near(0, near_2, 0) + near(0, near_2_other, 1)
    coded_2 = contract(pos, cd_tiles, integrals, blocks, heights[1:], coded_2)
    far_2 = after(far_2, coded_2)
    far_2_other = swap(far_2)
    blocks = far(0, far_2, 0) + far(0, far_2_other, 1)
    coded_2 = contract(pos, cd_tiles, integrals, blocks, heights[1:], coded_2)
    met_2 = along_x(coded_2)

    sums = add_second(pos, met_2, add_first(after(met_1, coded_2)))
    return add_last([sums[0]] + [shift(sums[s], "z", NZ, s) for s in (4, 1, 3, 5, 2, 6, 7)])


def solution(mesh):
    fine = Mesh(mesh.devices.reshape(NY, NC, NX, NZ), ("y", "c", "x", "z"))
    return jax.shard_map(
        per_device,
        mesh=fine,
        in_specs=(P(("y", "c"), ("x", "z")), P(("y", "c"), ("x", "z")), P(("y", "c"), ("x", "z"))),
        out_specs=P(("x", "z"), ("y", "c")),
        check_vma=False,
    )
```
